128 devices in a mesh: grid: 8 (over z, core), line: 16 (over x, y).
Axes of the slice: x: 4, y: 4, z: 4, core: 2. Of those that a mesh axis runs over, the one named last changes fastest.
Arguments:
- les: float32 [24, 8, 2048], P(None, 'grid', 'line'), may hold values from -6 to 6
- lines: float32 [8, 16, 128, 24, 128], P('grid', 'line'), may hold values from -6 to 6
- triplet_start: int32 [2, 8, 16, 128], P(None, 'grid', 'line'), may hold values from 0 to 80
- splice_owner: int32 [2, 8, 16, 128, 1], P(None, 'grid', 'line'), may hold values from 0 to 127; in each aligned block of 128 rows (0 to 127, 128 to 255, ..., all dimensions but the last counted through in order) at most 2 rows name the same one
- splice_line: int32 [2, 8, 16, 128], P(None, 'grid', 'line'), may hold values from 0 to 127
- splice_from: int32 [2, 8, 16, 128], P(None, 'grid', 'line'), may hold values from 0 to 7
- splice_to: int32 [2, 8, 16, 128], P(None, 'grid', 'line'), may hold values from 0 to 7
- chem_counts: int32 [8, 16, 128], P('grid', 'line'), may hold values from 1 to 6, as said below
- diffusivity: float32 [24], replicated, may hold values from 0.5 to 20
- rates: float32 [24, 24], replicated, may hold values from -1.25 to 1.25
- frozen_inverse: float32 [24, 24], replicated, may hold values from -0.3 to 0.5
Outputs:
- les_out: float32 [24, 8, 2048], P(None, 'grid', 'line')
- lines_out: float32 [8, 16, 128, 24, 128], P('grid', 'line')
The draws below stay inside these ranges and needn't reach their ends.
Inputs may be any that keep to these rules, and one draw needn't show every extreme that they name: `splice_owner`: in the rows of one device and one step no owner is named more than 2 times, a bound that some block reaches. `chem_counts`: some line has 6 substeps.
All inputs are finite; a program needn't handle non-finite values.
Results may differ from the reference program's by a relative error of at most 0.0003.
Values sent between devices are 32-bit elements; how exact they have to be, the bound alone decides.
No kernel may reach another device: no remote copies, remote signals or barrier semaphores. Data moves between devices by JAX's collectives and lax.ppermute only.
A program may use at most 64 MiB of HBM per device.

```python
import math
import jax
import jax.numpy as jnp
import numpy as np
from jax import lax

S = 24
P_SIZE = 128
SEG = 16
TRIP = 48
KMAX = 6
STEPS = 2
CX = 1
CY = 128
LINES_DEV = 128
NX = 8
NY = 2048
NSEG = 8
CAP = 2
N_GRID = 8
N_LINE = 16
DEVICES = 128


def draw_chem_counts(key, part):
    first = jax.random.fold_in(key, 11)
    second = jax.random.fold_in(key, 12)
    ceiling = jax.random.randint(first, (N_GRID, N_LINE, 1), 1, KMAX + 1)
    ceiling = ceiling.at[0, 0, 0].set(KMAX)
    counts = 1 + jax.random.randint(second, (N_GRID, N_LINE, LINES_DEV), 0, ceiling)
    counts = counts.at[0, 0, 0].set(KMAX)
    return counts.astype(jnp.int32)


def draw_frozen_inverse(key, part):
    first = jax.random.fold_in(key, 21)
    second = jax.random.fold_in(key, 22)
    diagonal = jax.random.uniform(first, (S,), jnp.float32, 0.2, 0.5)
    off_diag = jnp.clip(0.06 * jax.random.normal(second, (S, S), jnp.float32), -0.3, 0.3)
    ident = jnp.eye(S, dtype=jnp.float32)
    return (ident * diagonal[None, :] + (1.0 - ident) * off_diag).astype(jnp.float32)


def plant(values, rng, smallest, high):
    shape = values.shape
    spot = [jax.random.randint(jax.random.fold_in(rng, axis), (), 0, shape[axis]) for axis in range(len(shape))]
    values = values.at[tuple(spot)].set(smallest)
    longest = shape.index(max(shape))
    spot[longest] = (spot[longest] + 1) % shape[longest]
    return values.at[tuple(spot)].set(high)


def block_levels(key, extent, shards, smallest, largest):
    factor_of = 1.0
    for axis_at, blocks in shards:
        heights = jax.random.uniform(jax.random.fold_in(jax.random.fold_in(key, 6), axis_at), (blocks,), jnp.float32, smallest / len(shards), largest / len(shards))
        factor_of = factor_of * jnp.repeat(jnp.exp(heights), extent[axis_at] // blocks).reshape((-1,) + (1,) * (len(extent) - 1 - axis_at))
    return factor_of


def routed_block(own_key, own, number, rows, count, top, limit, slope):
    sequence = jax.random.permutation(own_key, count)
    crowded, common = load_shares(count, rows * top, limit, slope, True), load_shares(count, rows * top, limit, slope, False)
    places = jnp.arange(count)

    def named(sizes, turn):
        used = int((sizes > 0).sum())
        fixed = max(1, used // 4)
        passed = fixed + (places - fixed + turn * (used - fixed)) % max(1, count - fixed)
        return jnp.zeros((count,), jnp.int32).at[sequence[jnp.where(places < fixed, places, passed)]].set(jnp.asarray(sizes, jnp.int32))

    sizes = jnp.where(number % 4 == 0, named(crowded, number // 4), named(common, number - number // 4 - 1))
    mixed = jax.random.permutation(jax.random.fold_in(own, 3), count)
    donor, receiver = mixed[0:count // 2 * 2:2], mixed[1:count // 2 * 2:2]
    room = jnp.minimum(sizes[donor] - 1, limit - sizes[receiver]) // 2
    room = jnp.where((donor == sequence[0]) | (receiver == sequence[0]) | (sizes[receiver] == 0), 0, jnp.maximum(room, 0))
    passed = jax.random.randint(jax.random.fold_in(own, 4), (count // 2,), 0, 1 << 20) % (room + 1)
    sizes = sizes.at[donor].add(-passed).at[receiver].add(passed)
    labels = jnp.searchsorted(jnp.cumsum(sizes), jnp.arange(rows * top), side="right").astype(jnp.int32)
    listing = labels.reshape(top, rows).T
    listing = listing[jax.random.permutation(jax.random.fold_in(own, 1), rows)]
    turn = jax.random.randint(jax.random.fold_in(own, 2), (rows, 1), 0, top)
    return jnp.take_along_axis(listing, (jnp.arange(top)[None, :] + turn) % top, axis=1)


def load_shares(number_of, total, most, slope, full):
    loads = [(1 << 20) // math.isqrt(grade ** slope) + 1 for grade in range(1, number_of + 1)]
    largest = most if full else min(most, max(-(-total // number_of), total * loads[0] // sum(loads)))
    least = 1 if total - largest >= number_of - 1 else 0
    given, spare = [largest] + [least] * (number_of - 1), total - largest - least * (number_of - 1)
    while spare > 0:
        free = [i for i in range(1, number_of) if given[i] < largest] or [i for i in range(1, number_of) if given[i] < most]
        pool, left = sum([loads[i] for i in free]), spare
        for i in free:
            addition = min(most - given[i], max(1, left * loads[i] // pool), spare)
            given[i] = given[i] + addition
            spare = spare - addition
    return np.array(given)


def centred(rng, dims, width, bound, shards=(), held_as=jnp.bfloat16):
    drawn = width * jax.random.normal(rng, dims, jnp.float32)
    if shards:
        drawn = drawn * block_levels(rng, dims, shards, -0.22, 0.18)
    return jnp.clip(drawn, -bound, bound).astype(held_as)


def setup_inputs(seed: int = 0) -> dict:
    key_of = jax.random.split(jax.random.key(seed), 12)
    les = centred(key_of[0], (S, NX, NY), 1.0, 6.0, ((1, 8), (2, 16)), jnp.float32)
    lines = centred(key_of[1], (N_GRID, N_LINE, LINES_DEV, S, P_SIZE), 1.0, 6.0, ((0, 8), (1, 16)), jnp.float32)
    triplet_start = plant(jax.random.randint(key_of[2], (STEPS, N_GRID, N_LINE, LINES_DEV), 0, P_SIZE - TRIP + 1), jax.random.fold_in(key_of[2], 1), 0, P_SIZE - TRIP).astype(jnp.int32)
    splice_owner_keys = jax.random.split(jax.random.fold_in(key_of[3], 1), STEPS * N_GRID * N_LINE * LINES_DEV // LINES_DEV)
    splice_owner_turns = jax.random.permutation(jax.random.fold_in(key_of[3], 3), STEPS * N_GRID * N_LINE * LINES_DEV // LINES_DEV)
    splice_owner = jax.vmap(lambda own, number: routed_block(jax.random.fold_in(key_of[3], 2), own, number, LINES_DEV, DEVICES, 1, CAP, 2))(splice_owner_keys, splice_owner_turns).reshape((STEPS, N_GRID, N_LINE, LINES_DEV, 1))
    splice_line = plant(jax.random.randint(key_of[4], (STEPS, N_GRID, N_LINE, LINES_DEV), 0, LINES_DEV), jax.random.fold_in(key_of[4], 1), 0, LINES_DEV - 1).astype(jnp.int32)
    splice_from = plant(jax.random.randint(key_of[5], (STEPS, N_GRID, N_LINE, LINES_DEV), 0, NSEG), jax.random.fold_in(key_of[5], 1), 0, NSEG - 1).astype(jnp.int32)
    splice_to = plant(jax.random.randint(key_of[6], (STEPS, N_GRID, N_LINE, LINES_DEV), 0, NSEG), jax.random.fold_in(key_of[6], 1), 0, NSEG - 1).astype(jnp.int32)
    chem_counts = draw_chem_counts(jax.random.fold_in(key_of[11], 71), 0)
    diffusivity = jnp.clip(jnp.exp(jax.random.uniform(key_of[8], (S,), jnp.float32, math.log(0.5), math.log(20.0))), 0.5, 20.0)
    rates = centred(key_of[9], (S, S), S ** -0.5, 1.25, (), jnp.float32)
    frozen_inverse = draw_frozen_inverse(jax.random.fold_in(key_of[11], 71), 0)
    return dict(les=les, lines=lines, triplet_start=triplet_start, splice_owner=splice_owner, splice_line=splice_line, splice_from=splice_from, splice_to=splice_to, chem_counts=chem_counts, diffusivity=diffusivity, rates=rates, frozen_inverse=frozen_inverse)


les_rate = 0.2
relax_rate = 0.5
splice_weight = 0.5

def diffusion_inverse(diffusivity, points):
    place = jnp.arange(points)
    ends = ((place == 0) | (place == points - 1)).astype(jnp.float32)
    coeff = diffusivity[:, None]
    main = 1.0 + coeff * (2.0 - ends[None, :])
    off_diag = -coeff * jnp.ones((1, points), jnp.float32)
    lower = jnp.where(place[None, :] == 0, jnp.float32(0.0), off_diag)
    upper = jnp.where(place[None, :] == points - 1, jnp.float32(0.0), off_diag)
    ident = jnp.broadcast_to(jnp.eye(points, dtype=jnp.float32), (diffusivity.shape[0], points, points))
    return lax.linalg.tridiagonal_solve(lower, main, upper, ident)

def triplet_index(start, points, length):
    place = jnp.arange(points).astype(jnp.int32)
    rel = place[None, :] - start[:, None].astype(jnp.int32)
    third = length // 3
    source = jnp.where(rel < third, 3 * rel, jnp.where(rel < 2 * third, 3 * (2 * third - 1 - rel) + 1, 3 * (rel - 2 * third) + 2))
    inside = (rel >= 0) & (rel < length)
    return jnp.where(inside, source + start[:, None].astype(jnp.int32), place[None, :]).astype(jnp.int32)

def chemistry(state, counts, rates, frozen_inverse):
    for sub in range(KMAX):
        active = (counts > sub)[:, None, None]
        source = jnp.einsum('st,ltp->lsp', rates, jnp.tanh(state), precision=lax.Precision.HIGHEST)
        change = jnp.einsum('st,ltp->lsp', frozen_inverse, source, precision=lax.Precision.HIGHEST)
        state = jnp.where(active, state + change, state)
    return state

def reference(les, lines, triplet_start, splice_owner, splice_line, splice_from, splice_to, chem_counts, diffusivity, rates, frozen_inverse):
    inverse = diffusion_inverse(diffusivity, P_SIZE)
    total = N_GRID * N_LINE * LINES_DEV
    field = les
    state = lines.reshape(total, S, P_SIZE)
    counts = chem_counts.reshape(total)
    rows = jnp.arange(total).astype(jnp.int32)
    for step in range(STEPS):
        padded = jnp.pad(field, ((0, 0), (1, 1), (1, 1)))
        beside = padded[:, 2:, 1:-1] + padded[:, :-2, 1:-1] + padded[:, 1:-1, 2:] + padded[:, 1:-1, :-2]
        mid = field + les_rate * (beside - 4.0 * field)
        cellwise = mid.reshape(S, N_GRID, CX, N_LINE, CY).transpose(1, 3, 2, 4, 0).reshape(total, S)
        state = state + relax_rate * (cellwise - jnp.mean(state, axis=2))[:, :, None]
        index = triplet_index(triplet_start[step].reshape(total), P_SIZE, TRIP)
        state = jnp.take_along_axis(state, index[:, None, :], axis=2)
        state = jnp.einsum('lsp,sqp->lsq', state, inverse, precision=lax.Precision.HIGHEST)
        state = chemistry(state, counts, rates, frozen_inverse)
        four = state.reshape(total, S, NSEG, SEG)
        outgoing = four[rows, :, splice_from[step].reshape(total).astype(jnp.int32), :]
        target = (splice_owner[step].reshape(total) * LINES_DEV + splice_line[step].reshape(total)).astype(jnp.int32)
        landing = splice_to[step].reshape(total).astype(jnp.int32)
        previous = four[target, :, landing, :]
        four = four.at[target, :, landing, :].add(splice_weight * (outgoing - previous))
        state = four.reshape(total, S, P_SIZE)
        filtered = jnp.mean(state, axis=2)
        back = filtered.reshape(N_GRID, N_LINE, CX, CY, S).transpose(4, 0, 2, 1, 3).reshape(S, NX, NY)
        field = 0.5 * mid + 0.5 * back
    return (field, state.reshape(lines.shape))
```

```python
import jax
import jax.numpy as jnp
import numpy as np
from jax import lax
from jax.experimental import pallas as pl
from jax.experimental.pallas import tpu as pltpu
from jax.sharding import PartitionSpec as P

SEG = 16
TRIP = 48
KMAX = 6
STEPS = 2
LES_RATE = 0.2
SPECIES = 24
POINTS = 128
LINES = 128
OWNERS = 128
ROWS = 8
F32 = jnp.float32
BF16 = jnp.bfloat16


def cosine_tables():
    k = np.arange(POINTS)[:, None]
    p = np.arange(POINTS)[None, :]
    basis = np.sqrt(2.0 / POINTS) * np.cos(np.pi * k * (2 * p + 1) / (2 * POINTS))
    basis[0] = 1.0 / np.sqrt(POINTS)
    tables = []
    for table in (basis.T, basis):
        high = table.astype(BF16)
        low = (table - high.astype(np.float64)).astype(BF16)
        half = np.concatenate([high, low], axis=1)
        tables.append(np.concatenate([half, half], axis=0))
    eigen = 4.0 * np.sin(np.pi * np.arange(POINTS) / (2 * POINTS)) ** 2
    return tables[0], tables[1], eigen.astype(np.float32)[None, :]


def halves(value):
    high = value.astype(BF16)
    return high, (value - high.astype(F32)).astype(BF16)


def dot(a, b):
    return jnp.dot(a, b, preferred_element_type=F32)


def iota(axis, shape=(LINES, POINTS)):
    return lax.broadcasted_iota(jnp.int32, shape, axis)


def column(row):
    return jnp.transpose(jnp.broadcast_to(row.astype(F32), (LINES, POINTS)))


def lane_pick(value, index):
    return jnp.take_along_axis(value, index, axis=1, mode="promise_in_bounds")


def mix_tables(rates, frozen, high_ref, low_ref):
    exact = dict(precision=lax.Precision.HIGHEST, preferred_element_type=F32)
    matrix = jnp.dot(frozen, rates, **exact)
    side = SPECIES * 8
    spread = (iota(0, (side, SPECIES)) // 8 == iota(1, (side, SPECIES))).astype(F32)
    gather = (iota(0, (SPECIES, side)) == iota(1, (SPECIES, side)) // 8).astype(F32)
    wide = jnp.dot(jnp.dot(spread, matrix, **exact), gather, **exact)
    same = iota(0, (side, side)) % 8 == iota(1, (side, side)) % 8
    high, low = halves(jnp.where(same, wide, 0.0))
    high_ref[...] = high
    low_ref[...] = low


def middle(les, north, south, west, east):
    lane = iota(1, (SPECIES, LINES))
    left = jnp.where(lane == 0, pltpu.roll(west, 1, 1), pltpu.roll(les, 1, 1))
    right = jnp.where(lane == LINES - 1, pltpu.roll(east, LINES - 1, 1), pltpu.roll(les, LINES - 1, 1))
    return les + LES_RATE * (north + south + left + right - 4.0 * les)


def turned(value):
    pad = jnp.zeros((POINTS - SPECIES, LINES), F32)
    return jnp.transpose(jnp.concatenate([value, pad], axis=0))


def triplet_index(start):
    place = iota(1)
    start = start.astype(jnp.int32)
    rel = place - start
    third = TRIP // 3
    source = jnp.where(
        rel < third,
        3 * rel,
        jnp.where(rel < 2 * third, 3 * (2 * third - 1 - rel) + 1, 3 * (rel - 2 * third) + 2),
    )
    return jnp.where((rel >= 0) & (rel < TRIP), source + start, place)


def mixing(read, start_row, mid, diffusivity_ref, eigen_ref, first_ref, second_ref, state_ref, index_ref, shift_ref):
    index_ref[...] = triplet_index(column(start_row))
    shift_ref[...] = turned(0.5 * mid)
    lane = iota(1, (1, POINTS))

    def one(s, carry):
        value = lane_pick(read(s), index_ref[...])
        high, low = halves(value)
        wide = dot(jnp.concatenate([high, low], axis=1), first_ref[...])
        scale = 1.0 / (1.0 + diffusivity_ref[s] * eigen_ref[...])
        scale = jnp.where(lane == 0, 0.5, scale)
        high, low = halves((wide[:, :POINTS] + wide[:, POINTS:]) * scale)
        wide = dot(jnp.concatenate([high, low], axis=1), second_ref[...])
        shift = lane_pick(shift_ref[...], jnp.full((LINES, POINTS), s, jnp.int32))
        state_ref[s] = wide[:, :POINTS] + wide[:, POINTS:] + shift
        return carry

    lax.fori_loop(0, SPECIES, one, 0, unroll=2)


def chemistry(counts_row, high_ref, low_ref, state_ref, counts_ref):
    counts_ref[...] = column(counts_row)
    side = SPECIES * 8

    def substep(sub, carry):
        turn = sub.astype(F32)
        for unit in range(LINES // 16):
            parts = [slice(16 * unit, 16 * unit + 8), slice(16 * unit + 8, 16 * unit + 16)]
            old = [state_ref[:, part, :].reshape(side, POINTS) for part in parts]
            high, low = halves(jnp.tanh(jnp.concatenate(old, axis=1)))
            change = dot(high_ref[...], high) + (dot(low_ref[...], high) + dot(high_ref[...], low))
            for at, part in enumerate(parts):
                active = (counts_ref[part, :] > turn)[None]
                before = old[at].reshape(SPECIES, 8, POINTS)
                after = before + change[:, at * POINTS : (at + 1) * POINTS].reshape(SPECIES, 8, POINTS)
                state_ref[:, part, :] = jnp.where(active, after, before)
        return carry

    lax.fori_loop(0, KMAX, substep, 0)


def packing(owner_row, line_row, from_row, to_row, state_ref, out_ref, send_ref):
    lane = iota(1)
    pick = column(from_row).astype(jnp.int32) * SEG + lane % SEG
    group = lane // SEG
    for third in range(3):
        gathered = jnp.zeros((LINES, POINTS), F32)
        for s in range(8):
            gathered = jnp.where(group == s, lane_pick(state_ref[8 * third + s], pick), gathered)
        high, low = halves(gathered)
        out_ref[:LINES, third * POINTS : (third + 1) * POINTS] = high
        out_ref[LINES:, third * POINTS : (third + 1) * POINTS] = low
    owner = column(owner_row).astype(jnp.int32)
    earlier = (owner == owner_row) & (iota(0) < lane)
    rank = jnp.sum(earlier.astype(F32), axis=0, keepdims=True)
    aims = jnp.where(lane < 64, column(line_row) + 1.0, column(to_row)).astype(BF16)
    for slot in range(2):
        placing = ((iota(0) == owner_row) & (rank == slot)).astype(F32).astype(BF16)
        sending = dot(jnp.concatenate([placing, placing], axis=1), out_ref[...])
        for third in range(3):
            send_ref[pl.ds(3 * slot + third, OWNERS, stride=ROWS), :] = sending[
                :, third * POINTS : (third + 1) * POINTS
            ]
        send_ref[pl.ds(6 + slot, OWNERS, stride=ROWS), :] = dot(placing, aims)


def splicing(received_ref, state_ref, write, parts_ref, place_ref, land_ref):
    lane = iota(1)
    for slot in range(2):
        aim = received_ref[pl.ds(6 + slot, OWNERS, stride=ROWS), :]
        line = jnp.broadcast_to(aim[:, :1], (OWNERS, LINES)).astype(jnp.int32) - 1
        segment = jnp.broadcast_to(aim[:, 64:65], (OWNERS, POINTS)).astype(jnp.int32)
        hit = jnp.transpose((line == lane).astype(F32)).astype(BF16)
        place_ref[:, slot * OWNERS : (slot + 1) * OWNERS] = hit
        place_ref[:, (2 + slot) * OWNERS : (3 + slot) * OWNERS] = hit
        land_ref[slot * OWNERS : (slot + 1) * OWNERS, :] = (segment == lane // SEG).astype(F32)
        for third in range(3):
            parts_ref[third, slot * OWNERS : (slot + 1) * OWNERS, :] = received_ref[
                pl.ds(3 * slot + third, OWNERS, stride=ROWS), :
            ]
    arrivals = dot(place_ref[:, : 2 * OWNERS], land_ref[...].astype(BF16))
    both = iota(1, (2 * OWNERS, POINTS)) % SEG

    def one(s, means):
        piece = lane_pick(parts_ref[s // 8], both + (s % 8) * SEG)
        high, low = halves(jnp.where(land_ref[...] > 0.5, piece, 0.0))
        gained = dot(place_ref[...], jnp.concatenate([high, low], axis=0))
        old = state_ref[s]
        new = old + 0.5 * (gained - arrivals * old)
        write(s, new)
        mean = jnp.sum(new, axis=1, keepdims=True) * (1.0 / POINTS)
        return jnp.where(lane == s, mean, means)

    means = lax.fori_loop(0, SPECIES, one, jnp.zeros((LINES, POINTS), F32), unroll=2)
    return jnp.transpose(means)[:SPECIES]


def step_kernel(
    step, first, lines_ref, les_ref, north_ref, south_ref, west_ref, east_ref, start_ref, owner_ref, line_ref, from_ref,
    to_ref, counts_ref, diffusivity_ref, eigen_ref, first_ref, second_ref, a_ref, b_ref, *rest,
):
    if first:
        state_ref, send_ref, mid_ref, high_ref, low_ref, index_ref, shift_ref, turns_ref, out_ref = rest
        mix_tables(a_ref[...], b_ref[...], high_ref, low_ref)

        def read(s):
            return lines_ref[pl.ds(s, LINES, stride=SPECIES), :]
    else:
        state_ref, send_ref, mid_ref, index_ref, shift_ref, turns_ref, out_ref = rest
        high_ref, low_ref = a_ref, b_ref

        def read(s):
            return lines_ref[s]

    mid = middle(les_ref[:, 0], north_ref[:, 0], south_ref[:, 0], west_ref[:, 0], east_ref[:, 0])
    mid_ref[...] = mid
    mixing(
        read, start_ref[step, 0], mid, diffusivity_ref, eigen_ref, first_ref, second_ref, state_ref, index_ref, shift_ref
    )
    chemistry(counts_ref[0], high_ref, low_ref, state_ref, turns_ref)
    packing(owner_ref[step, 0], line_ref[step, 0], from_ref[step, 0], to_ref[step, 0], state_ref, out_ref, send_ref)


def splice_kernel(last, received_ref, state_ref, mid_ref, les_ref, lines_ref, parts_ref, place_ref, land_ref):
    def write(s, value):
        if last:
            lines_ref[pl.ds(s, LINES, stride=SPECIES), :] = value
        else:
            lines_ref[s] = value

    means = splicing(received_ref, state_ref, write, parts_ref, place_ref, land_ref)
    les_ref[:, 0] = 0.5 * mid_ref[...] + 0.5 * means


VMEM = pl.BlockSpec(memory_space=pltpu.VMEM)
SMEM = pl.BlockSpec(memory_space=pltpu.SMEM)
STATE = jax.ShapeDtypeStruct((SPECIES, LINES, POINTS), F32)


def call(kernel, inputs, outputs, scratch, flops):
    shapes = [x for x in outputs]
    specs = [SMEM if smem else VMEM for _, smem in inputs]
    size = sum(x.size * x.dtype.itemsize for x, _ in inputs) + sum(x.size * x.dtype.itemsize for x in shapes)
    return pl.pallas_call(
        kernel,
        out_shape=shapes,
        in_specs=specs,
        out_specs=[VMEM] * len(shapes),
        scratch_shapes=scratch,
        cost_estimate=pl.CostEstimate(flops=flops, bytes_accessed=size, transcendentals=0),
        compiler_params=pltpu.CompilerParams(vmem_limit_bytes=40 << 20),
    )(*[x for x, _ in inputs])


def beside(field):
    around = []
    for axis in ("grid", "line"):
        peers = lax.axis_size(axis)
        up = [(i, i + 1) for i in range(peers - 1)]
        around.append(lax.ppermute(field, axis, up))
        around.append(lax.ppermute(field, axis, [(b, a) for a, b in up]))
    return around


def body(
    les,
    lines,
    triplet_start,
    splice_owner,
    splice_line,
    splice_from,
    splice_to,
    chem_counts,
    diffusivity,
    rates,
    frozen_inverse,
):
    first_table, second_table, eigen = (jnp.asarray(x) for x in cosine_tables())
    side = SPECIES * 8
    tables = [jax.ShapeDtypeStruct((side, side), BF16)] * 2
    send = jax.ShapeDtypeStruct((OWNERS * ROWS, POINTS), F32)
    mid_shape = jax.ShapeDtypeStruct((SPECIES, LINES), F32)
    owner = splice_owner.reshape(STEPS, 1, 1, LINES)
    field = les
    state = lines.reshape(LINES * SPECIES, POINTS)
    mix = (rates, frozen_inverse)
    for step in range(STEPS):
        last = step == STEPS - 1
        rim = beside(field)
        inputs = [(x, False) for x in (state, field, *rim, triplet_start, owner, splice_line, splice_from, splice_to, chem_counts)]
        inputs += [(diffusivity, True)] + [(x, False) for x in (eigen, first_table, second_table, *mix)]
        scratch = [
            pltpu.VMEM((LINES, POINTS), jnp.int32),
            pltpu.VMEM((LINES, POINTS), F32),
            pltpu.VMEM((LINES, POINTS), F32),
            pltpu.VMEM((2 * LINES, 3 * POINTS), BF16),
        ]
        first = step == 0

        def advance(*refs, step=step, first=first):
            step_kernel(step, first, *refs)

        outs = call(advance, inputs, [STATE, send, mid_shape] + (tables if first else []), scratch, 4 * 10**9)
        state, sending, mid = outs[:3]
        if first:
            mix = outs[3:]
        received = lax.all_to_all(
            sending.reshape(OWNERS, ROWS, POINTS), ("grid", "line"), split_axis=0, concat_axis=0, tiled=True
        ).reshape(OWNERS * ROWS, POINTS)
        scratch = [
            pltpu.VMEM((3, 2 * OWNERS, POINTS), F32),
            pltpu.VMEM((LINES, 4 * OWNERS), BF16),
            pltpu.VMEM((2 * OWNERS, POINTS), F32),
        ]
        after = jax.ShapeDtypeStruct((LINES * SPECIES, POINTS), F32) if last else STATE

        def land(*refs, last=last):
            splice_kernel(last, *refs)

        field, state = call(
            land, [(x, False) for x in (received, state, mid)], [jax.ShapeDtypeStruct(les.shape, F32), after], scratch, 10**9
        )
    return (field, state.reshape(lines.shape))


def solution(mesh):
    in_specs = (
        P(None, "grid", "line"),
        P("grid", "line", None, None, None),
        P(None, "grid", "line", None),
        P(None, "grid", "line", None, None),
        P(None, "grid", "line", None),
        P(None, "grid", "line", None),
        P(None, "grid", "line", None),
        P("grid", "line", None),
        P(),
        P(),
        P(),
    )
    out_specs = (P(None, "grid", "line"), P("grid", "line", None, None, None))
    return jax.shard_map(body, mesh=mesh, in_specs=in_specs, out_specs=out_specs, check_vma=False)
```

```python
import jax
import jax.numpy as jnp
import numpy as np
from jax import lax
from jax.experimental import pallas as pl
from jax.experimental.pallas import tpu as pltpu
from jax.sharding import PartitionSpec as P

SEG = 16
TRIP = 48
KMAX = 6
STEPS = 2
LES_RATE = 0.2
SPECIES = 24
POINTS = 128
LINES = 128
OWNERS = 128
ROWS = 8
F32 = jnp.float32
BF16 = jnp.bfloat16


def cosine_tables():
    k = np.arange(POINTS)[:, None]
    p = np.arange(POINTS)[None, :]
    basis = np.sqrt(2.0 / POINTS) * np.cos(np.pi * k * (2 * p + 1) / (2 * POINTS))
    basis[0] = 1.0 / np.sqrt(POINTS)
    tables = []
    for table in (basis.T, basis):
        high = table.astype(BF16)
        low = (table - high.astype(np.float64)).astype(BF16)
        half = np.concatenate([high, low], axis=1)
        tables.append(np.concatenate([half, half], axis=0))
    eigen = 4.0 * np.sin(np.pi * np.arange(POINTS) / (2 * POINTS)) ** 2
    return tables[0], tables[1], eigen.astype(np.float32)[None, :]


def halves(value):
    high = value.astype(BF16)
    return high, (value - high.astype(F32)).astype(BF16)


def dot(a, b):
    return jnp.dot(a, b, preferred_element_type=F32)


def iota(axis, shape=(LINES, POINTS)):
    return lax.broadcasted_iota(jnp.int32, shape, axis)


def column(row):
    return jnp.transpose(jnp.broadcast_to(row.astype(F32), (LINES, POINTS)))


def lane_pick(value, index):
    return jnp.take_along_axis(value, index, axis=1, mode="promise_in_bounds")


def mix_tables(rates, frozen, high_ref, low_ref):
    exact = dict(precision=lax.Precision.HIGHEST, preferred_element_type=F32)
    matrix = jnp.dot(frozen, rates, **exact)
    side = SPECIES * 8
    spread = (iota(0, (side, SPECIES)) // 8 == iota(1, (side, SPECIES))).astype(F32)
    gather = (iota(0, (SPECIES, side)) == iota(1, (SPECIES, side)) // 8).astype(F32)
    wide = jnp.dot(jnp.dot(spread, matrix, **exact), gather, **exact)
    same = iota(0, (side, side)) % 8 == iota(1, (side, side)) % 8
    high, low = halves(jnp.where(same, wide, 0.0))
    high_ref[...] = high
    low_ref[...] = low


def middle(les, grid_even, grid_odd, line_even, line_odd):
    row, place = lax.axis_index("grid"), lax.axis_index("line")
    inner = jnp.logical_and(row > 0, row < lax.axis_size("grid") - 1)
    even = place % 2 == 0
    west = jnp.where(even, line_odd, line_even)
    east = jnp.where(even, line_even, line_odd)
    west = jnp.where(place > 0, west, 0.0)
    east = jnp.where(place < lax.axis_size("line") - 1, east, 0.0)
    lane = iota(1, (SPECIES, LINES))
    left = jnp.where(lane == 0, pltpu.roll(west, 1, 1), pltpu.roll(les, 1, 1))
    right = jnp.where(lane == LINES - 1, pltpu.roll(east, LINES - 1, 1), pltpu.roll(les, LINES - 1, 1))
    return les + LES_RATE * (grid_even + jnp.where(inner, grid_odd, 0.0) + left + right - 4.0 * les)


def turned(value):
    pad = jnp.zeros((POINTS - SPECIES, LINES), F32)
    return jnp.transpose(jnp.concatenate([value, pad], axis=0))


def triplet_index(start):
    place = iota(1)
    start = start.astype(jnp.int32)
    rel = place - start
    third = TRIP // 3
    source = jnp.where(
        rel < third,
        3 * rel,
        jnp.where(rel < 2 * third, 3 * (2 * third - 1 - rel) + 1, 3 * (rel - 2 * third) + 2),
    )
    return jnp.where((rel >= 0) & (rel < TRIP), source + start, place)


def mixing(read, start_row, scale_ref, first_ref, second_ref, state_ref, index_ref):
    index_ref[...] = triplet_index(column(start_row))
    group = 8

    def one(at, carry):
        species = [at * group + i for i in range(group)]
        value = jnp.concatenate([lane_pick(read(s), index_ref[...]) for s in species], axis=0)
        wide = dot(jnp.concatenate(halves(value), axis=1), first_ref[...])
        value = wide[:, :POINTS] + wide[:, POINTS:]
        value = value.reshape(group, LINES, POINTS)
        value = jnp.concatenate([value[i] * scale_ref[pl.ds(s, 1), :] for i, s in enumerate(species)], axis=0)
        wide = dot(jnp.concatenate(halves(value), axis=1), second_ref[...])
        value = (wide[:, :POINTS] + wide[:, POINTS:]).reshape(group, LINES, POINTS)
        for i, s in enumerate(species):
            state_ref[s] = value[i]
        return carry

    lax.fori_loop(0, SPECIES // group, one, 0)


def chemistry(counts_row, shift, high_ref, low_ref, mixed_ref, state_ref, counts_ref):
    counts_ref[...] = column(counts_row)
    side = SPECIES * 8

    def substep(turn, read):
        for unit in range(LINES // 16):
            parts = [slice(16 * unit, 16 * unit + 8), slice(16 * unit + 8, 16 * unit + 16)]
            old = [read(part).reshape(side, POINTS) for part in parts]
            high, low = halves(jnp.tanh(jnp.concatenate(old, axis=1)))
            change = dot(high_ref[...], high) + (dot(low_ref[...], high) + dot(high_ref[...], low))
            for at, part in enumerate(parts):
                active = (counts_ref[part, :] > turn)[None]
                before = old[at].reshape(SPECIES, 8, POINTS)
                after = before + change[:, at * POINTS : (at + 1) * POINTS].reshape(SPECIES, 8, POINTS)
                state_ref[:, part, :] = jnp.where(active, after, before)

    def shifted(part):
        rows = [jnp.broadcast_to(shift[part, s : s + 1], (8, POINTS))[None] for s in range(SPECIES)]
        return mixed_ref[:, part, :] + jnp.concatenate(rows, axis=0)

    substep(0.0, shifted)

    def later(sub, carry):
        substep(sub.astype(F32), lambda part: state_ref[:, part, :])
        return carry

    lax.fori_loop(1, KMAX, later, 0)


def packing(owner_row, line_row, from_row, to_row, state_ref, out_ref, send_ref):
    lane = iota(1)
    pick = column(from_row).astype(jnp.int32) * SEG + lane % SEG
    landing = column(to_row)
    group = (lane // SEG - landing.astype(jnp.int32)) & 7
    for third in range(3):
        gathered = jnp.zeros((LINES, POINTS), F32)
        for s in range(8):
            gathered = jnp.where(group == s, lane_pick(state_ref[8 * third + s], pick), gathered)
        high, low = halves(gathered)
        out_ref[:LINES, third * POINTS : (third + 1) * POINTS] = high
        out_ref[LINES:, third * POINTS : (third + 1) * POINTS] = low
    owner = column(owner_row).astype(jnp.int32)
    earlier = (owner == owner_row) & (iota(0) < lane)
    rank = jnp.sum(earlier.astype(F32), axis=0, keepdims=True)
    aims = jnp.where(lane < 64, column(line_row) + 1.0, landing).astype(BF16)
    for slot in range(2):
        placing = ((iota(0) == owner_row) & (rank == slot)).astype(F32).astype(BF16)
        sending = dot(jnp.concatenate([placing, placing], axis=1), out_ref[...])
        for third in range(3):
            send_ref[pl.ds(3 * slot + third, OWNERS, stride=ROWS), :] = sending[
                :, third * POINTS : (third + 1) * POINTS
            ]
        send_ref[pl.ds(6 + slot, OWNERS, stride=ROWS), :] = dot(placing, aims)


def splicing(received_ref, state_ref, write, parts_ref, hits_ref, gain_ref):
    place = iota(0).astype(F32)
    for slot in range(2):
        aim = jnp.transpose(received_ref[pl.ds(6 + slot, OWNERS, stride=ROWS), :])
        code = aim[64:65] * LINES + aim[:1] - 1.0
        rows = slice(slot * OWNERS, (slot + 1) * OWNERS)
        lows = slice((2 + slot) * OWNERS, (3 + slot) * OWNERS)
        for third in range(3):
            high, low = halves(received_ref[pl.ds(3 * slot + third, OWNERS, stride=ROWS), :])
            parts_ref[rows, third * POINTS : (third + 1) * POINTS] = high
            parts_ref[lows, third * POINTS : (third + 1) * POINTS] = low
        parts_ref[rows, 3 * POINTS :] = jnp.ones((OWNERS, POINTS), BF16)
        parts_ref[lows, 3 * POINTS :] = jnp.zeros((OWNERS, POINTS), BF16)
        for segment in range(8):
            hit = jnp.where(place + float(segment * LINES) == code, 0.5, 0.0).astype(BF16)
            hits_ref[segment * LINES : (segment + 1) * LINES, rows] = hit
            hits_ref[segment * LINES : (segment + 1) * LINES, lows] = hit
    gain_ref[...] = dot(hits_ref[...], parts_ref[...]).reshape(8, LINES, 4 * POINTS)
    group = iota(1, (8, POINTS)) // SEG
    bits = [(group & bit) != 0 for bit in (1, 2, 4)]

    def block(at, carry):
        first = pl.multiple_of(8 * at, 8)
        lines = pl.ds(first, 8)
        share = gain_ref[0, lines, 3 * POINTS :]
        for segment in range(1, 8):
            share = jnp.where(group == segment, gain_ref[segment, lines, 3 * POINTS :], share)
        keep = 1.0 - share
        for third in range(3):
            shifted = [gain_ref[segment, lines, third * POINTS : (third + 1) * POINTS] for segment in range(8)]
            for bit, mask in zip((1, 2, 4), bits):
                shifted = [jnp.where(mask, shifted[(i + bit) % 8], shifted[i]) for i in range(8)]
            for s in range(8):
                gained = shifted[-s % 8]
                if s:
                    gained = pltpu.roll(gained, POINTS - SEG * s, 1)
                write(8 * third + s, at, state_ref[8 * third + s, lines, :] * keep + gained)
        return carry

    lax.fori_loop(0, LINES // 8, block, 0, unroll=2)


def means_of(read):
    lane = iota(1)

    def one(s, means):
        return jnp.where(lane == s, jnp.sum(read(s), axis=1, keepdims=True) * (1.0 / POINTS), means)

    return jnp.transpose(lax.fori_loop(0, SPECIES, one, jnp.zeros((LINES, POINTS), F32), unroll=4))[:SPECIES]


def scales(diffusivity_row, eigen_row):
    row = jnp.concatenate([diffusivity_row, jnp.zeros((1, POINTS - SPECIES), F32)], axis=1)
    lane = iota(1, (SPECIES, POINTS))
    return jnp.where(lane == 0, 0.5, 1.0 / (1.0 + column(row)[:SPECIES] * eigen_row))


def first_mix_kernel(
    lines_hbm, start_hbm, diffusivity_hbm, eigen_hbm, first_hbm, second_hbm, rates_hbm, frozen_hbm,
    mixed_ref, high_ref, low_ref, scale_ref,
    lines_ref, start_ref, diffusivity_ref, eigen_ref, first_ref, second_ref, rates_ref, frozen_ref, index_ref, sems,
):
    here = (rates_ref, frozen_ref, diffusivity_ref, eigen_ref, start_ref, first_ref, second_ref, lines_ref)
    there = (rates_hbm, frozen_hbm, diffusivity_hbm, eigen_hbm, start_hbm, first_hbm, second_hbm, lines_hbm)
    copies = [pltpu.make_async_copy(a, b, sems.at[i]) for i, (a, b) in enumerate(zip(there, here))]
    for copy in reversed(copies):
        copy.start()
    for copy in copies[:5]:
        copy.wait()
    mix_tables(rates_ref[...], frozen_ref[...], high_ref, low_ref)
    scale_ref[...] = scales(diffusivity_ref[...], eigen_ref[...])
    for copy in copies[5:]:
        copy.wait()

    def read(s):
        return lines_ref[pl.ds(s, LINES, stride=SPECIES), :]

    mixing(read, start_ref[0, 0], scale_ref, first_ref, second_ref, mixed_ref, index_ref)


def next_mix_kernel(state_ref, start_ref, scale_ref, first_ref, second_ref, mixed_ref, index_ref):
    mixing(lambda s: state_ref[s], start_ref[1, 0], scale_ref, first_ref, second_ref, mixed_ref, index_ref)


def react_kernel(
    step, mixed_ref, les_ref, grid_even_ref, grid_odd_ref, line_even_ref, line_odd_ref, owner_ref, line_ref, from_ref,
    to_ref, counts_ref, high_ref, low_ref, state_ref, send_ref, mid_ref, turns_ref, out_ref,
):
    mid = middle(les_ref[:, 0], grid_even_ref[:, 0], grid_odd_ref[:, 0], line_even_ref[:, 0], line_odd_ref[:, 0])
    mid_ref[...] = mid
    chemistry(counts_ref[0], turned(0.5 * mid), high_ref, low_ref, mixed_ref, state_ref, turns_ref)
    packing(owner_ref[step, 0], line_ref[step, 0], from_ref[step, 0], to_ref[step, 0], state_ref, out_ref, send_ref)


def next_splice_kernel(received_ref, state_ref, mid_ref, les_ref, lines_ref, parts_ref, hits_ref, gain_ref):
    def write(species, at, value):
        lines_ref[species, pl.ds(pl.multiple_of(8 * at, 8), 8), :] = value

    splicing(received_ref, state_ref, write, parts_ref, hits_ref, gain_ref)
    les_ref[:, 0] = 0.5 * mid_ref[...] + 0.5 * means_of(lambda s: lines_ref[s])


def last_splice_kernel(
    received_ref, state_ref, mid_ref, les_ref, lines_hbm, parts_ref, hits_ref, gain_ref, lines_ref, sems
):
    rows = 8 * SPECIES

    def out(at):
        part = pl.ds(pl.multiple_of(at * rows, rows), rows)
        return pltpu.make_async_copy(lines_ref.at[part], lines_hbm.at[part], sems.at[at])

    def write(species, at, value):
        lines_ref[pl.ds(at * rows + species, 8, stride=SPECIES), :] = value
        if species == SPECIES - 1:
            out(at).start()

    splicing(received_ref, state_ref, write, parts_ref, hits_ref, gain_ref)
    means = means_of(lambda s: lines_ref[pl.ds(s, LINES, stride=SPECIES), :])
    les_ref[:, 0] = 0.5 * mid_ref[...] + 0.5 * means
    for at in range(LINES // 8):
        out(at).wait()


VMEM = pl.BlockSpec(memory_space=pltpu.VMEM)
HBM = pl.BlockSpec(memory_space=pltpu.HBM)
STATE = jax.ShapeDtypeStruct((SPECIES, LINES, POINTS), F32)
FLAT = jax.ShapeDtypeStruct((LINES * SPECIES, POINTS), F32)
SPLICE_SCRATCH = [
    pltpu.VMEM((4 * OWNERS, 4 * POINTS), BF16),
    pltpu.VMEM((8 * LINES, 4 * OWNERS), BF16),
    pltpu.VMEM((8, LINES, 4 * POINTS), F32),
]


def call(kernel, inputs, outputs, scratch, micros, in_space=VMEM, out_specs=None):
    size = sum(x.size * x.dtype.itemsize for x in [*inputs, *outputs])
    if in_space is HBM:
        inputs = [pltpu.with_memory_space_constraint(x, pltpu.HBM) for x in inputs]
    return pl.pallas_call(
        kernel,
        out_shape=outputs,
        in_specs=[in_space] * len(inputs),
        out_specs=out_specs or [VMEM] * len(outputs),
        scratch_shapes=scratch,
        cost_estimate=pl.CostEstimate(flops=micros * 10**9, bytes_accessed=size, transcendentals=0),
        compiler_params=pltpu.CompilerParams(vmem_limit_bytes=32 << 20),
    )(*inputs)


def beside(field):
    around = []
    for axis in ("grid", "line"):
        peers = lax.axis_size(axis)
        for start in (0, 1):
            pairs = [(i, (i + 1) % peers) for i in range(start, peers, 2)]
            around.append(lax.ppermute(field, axis, pairs + [(b, a) for a, b in pairs]))
    return around


def body(
    les,
    lines,
    triplet_start,
    splice_owner,
    splice_line,
    splice_from,
    splice_to,
    chem_counts,
    diffusivity,
    rates,
    frozen_inverse,
):
    first_table, second_table, eigen = (jnp.asarray(x) for x in cosine_tables())
    side = SPECIES * 8
    send = jax.ShapeDtypeStruct((OWNERS * ROWS, POINTS), F32)
    plane = jax.ShapeDtypeStruct((SPECIES, LINES), F32)
    table = jax.ShapeDtypeStruct((side, side), BF16)
    owner = splice_owner.reshape(STEPS, 1, 1, LINES)
    field = les
    index = pltpu.VMEM((LINES, POINTS), jnp.int32)
    for step in range(STEPS):
        last = step == STEPS - 1
        rim = beside(field)
        if step == 0:
            inputs = [lines.reshape(FLAT.shape), triplet_start, diffusivity.reshape(1, SPECIES), eigen]
            inputs += [first_table, second_table, rates, frozen_inverse]
            scratch = [pltpu.VMEM(x.shape, x.dtype) for x in inputs] + [index, pltpu.SemaphoreType.DMA((len(inputs),))]
            mixed, high, low, scale = call(
                first_mix_kernel, inputs, [STATE, table, table, plane], scratch, 4, in_space=HBM
            )
        else:
            inputs = [state, triplet_start, scale, first_table, second_table]
            (mixed,) = call(next_mix_kernel, inputs, [STATE], [index], 3)

        def react(*refs, step=step):
            react_kernel(step, *refs)

        inputs = [mixed, field, *rim, owner, splice_line, splice_from, splice_to, chem_counts, high, low]
        scratch = [pltpu.VMEM((LINES, POINTS), F32), pltpu.VMEM((2 * LINES, 3 * POINTS), BF16)]
        state, sending, mid = call(react, inputs, [STATE, send, plane], scratch, 8)
        received = lax.all_to_all(
            sending.reshape(OWNERS, ROWS, POINTS), ("grid", "line"), split_axis=0, concat_axis=0, tiled=True
        ).reshape(OWNERS * ROWS, POINTS)
        inputs = [received, state, mid]
        outputs = [jax.ShapeDtypeStruct(les.shape, F32), FLAT if last else STATE]
        if last:
            scratch = SPLICE_SCRATCH + [pltpu.VMEM(FLAT.shape, F32), pltpu.SemaphoreType.DMA((LINES // 8,))]
            field, state = call(last_splice_kernel, inputs, outputs, scratch, 3, out_specs=[VMEM, HBM])
        else:
            field, state = call(next_splice_kernel, inputs, outputs, SPLICE_SCRATCH, 3)
    return (field, state.reshape(lines.shape))


def solution(mesh):
    in_specs = (
        P(None, "grid", "line"),
        P("grid", "line", None, None, None),
        P(None, "grid", "line", None),
        P(None, "grid", "line", None, None),
        P(None, "grid", "line", None),
        P(None, "grid", "line", None),
        P(None, "grid", "line", None),
        P("grid", "line", None),
        P(),
        P(),
        P(),
    )
    out_specs = (P(None, "grid", "line"), P("grid", "line", None, None, None))
    return jax.shard_map(body, mesh=mesh, in_specs=in_specs, out_specs=out_specs, check_vma=False)
```

```python
import jax
import jax.numpy as jnp
import numpy as np
from jax import lax
from jax.experimental import pallas as pl
from jax.experimental.pallas import tpu as pltpu
from jax.sharding import PartitionSpec as P

SEG = 16
TRIP = 48
KMAX = 6
STEPS = 2
LES_RATE = 0.2
SPECIES = 24
POINTS = 128
LINES = 128
OWNERS = 128
ROWS = 8
F32 = jnp.float32
BF16 = jnp.bfloat16


def cosine_tables():
    k = np.arange(POINTS)[:, None]
    p = np.arange(POINTS)[None, :]
    basis = np.sqrt(2.0 / POINTS) * np.cos(np.pi * k * (2 * p + 1) / (2 * POINTS))
    basis[0] = 1.0 / np.sqrt(POINTS)
    tables = []
    for table in (basis.T, basis):
        high = table.astype(BF16)
        low = (table - high.astype(np.float64)).astype(BF16)
        half = np.concatenate([high, low], axis=1)
        tables.append(np.concatenate([half, half], axis=0))
    eigen = 4.0 * np.sin(np.pi * np.arange(POINTS) / (2 * POINTS)) ** 2
    return tables[0], tables[1], eigen.astype(np.float32)[None, :]


def halves(value):
    high = value.astype(BF16)
    return high, (value - high.astype(F32)).astype(BF16)


def dot(a, b):
    return jnp.dot(a, b, preferred_element_type=F32)


def iota(axis, shape=(LINES, POINTS)):
    return lax.broadcasted_iota(jnp.int32, shape, axis)


def column(row):
    return jnp.transpose(jnp.broadcast_to(row.astype(F32), (LINES, POINTS)))


def lane_pick(value, index):
    return jnp.take_along_axis(value, index, axis=1, mode="promise_in_bounds")


def mix_tables(rates, frozen, high_ref, low_ref):
    exact = dict(precision=lax.Precision.HIGHEST, preferred_element_type=F32)
    matrix = jnp.dot(frozen, rates, **exact)
    side = SPECIES * 8
    spread = (iota(0, (side, SPECIES)) // 8 == iota(1, (side, SPECIES))).astype(F32)
    gather = (iota(0, (SPECIES, side)) == iota(1, (SPECIES, side)) // 8).astype(F32)
    wide = jnp.dot(jnp.dot(spread, matrix, **exact), gather, **exact)
    same = iota(0, (side, side)) % 8 == iota(1, (side, side)) % 8
    high, low = halves(jnp.where(same, wide, 0.0))
    high_ref[...] = high
    low_ref[...] = low


def middle(les, grid_even, grid_odd, line_even, line_odd):
    row, place = lax.axis_index("grid"), lax.axis_index("line")
    inner = jnp.logical_and(row > 0, row < lax.axis_size("grid") - 1)
    even = place % 2 == 0
    west = jnp.where(even, line_odd, line_even)
    east = jnp.where(even, line_even, line_odd)
    west = jnp.where(place > 0, west, 0.0)
    east = jnp.where(place < lax.axis_size("line") - 1, east, 0.0)
    lane = iota(1, (SPECIES, LINES))
    left = jnp.where(lane == 0, pltpu.roll(west, 1, 1), pltpu.roll(les, 1, 1))
    right = jnp.where(lane == LINES - 1, pltpu.roll(east, LINES - 1, 1), pltpu.roll(les, LINES - 1, 1))
    return les + LES_RATE * (grid_even + jnp.where(inner, grid_odd, 0.0) + left + right - 4.0 * les)


def turned(value):
    pad = jnp.zeros((POINTS - SPECIES, LINES), F32)
    return jnp.transpose(jnp.concatenate([value, pad], axis=0))


def triplet_index(start):
    place = iota(1)
    start = start.astype(jnp.int32)
    rel = place - start
    third = TRIP // 3
    source = jnp.where(
        rel < third,
        3 * rel,
        jnp.where(rel < 2 * third, 3 * (2 * third - 1 - rel) + 1, 3 * (rel - 2 * third) + 2),
    )
    return jnp.where((rel >= 0) & (rel < TRIP), source + start, place)


def mixing(read, start_row, scale_ref, first_ref, second_ref, state_ref, index_ref, ready=None):
    index_ref[...] = triplet_index(column(start_row))
    group = 8

    for at in range(SPECIES // group):
        species = [at * group + i for i in range(group)]
        if ready is not None:
            ready(at)
        value = jnp.concatenate([lane_pick(read(s), index_ref[...]) for s in species], axis=0)
        wide = dot(jnp.concatenate(halves(value), axis=1), first_ref[...])
        value = wide[:, :POINTS] + wide[:, POINTS:]
        value = value.reshape(group, LINES, POINTS)
        value = jnp.concatenate([value[i] * scale_ref[s : s + 1, :] for i, s in enumerate(species)], axis=0)
        wide = dot(jnp.concatenate(halves(value), axis=1), second_ref[...])
        value = (wide[:, :POINTS] + wide[:, POINTS:]).reshape(group, LINES, POINTS)
        for i, s in enumerate(species):
            state_ref[s] = value[i]


def chemistry(counts_row, shift, high_ref, low_ref, mixed_ref, state_ref, counts_ref, finish):
    counts_ref[...] = column(counts_row)
    side = SPECIES * 8

    def shifted(part):
        rows = [jnp.broadcast_to(shift[part, s : s + 1], (8, POINTS))[None] for s in range(SPECIES)]
        return mixed_ref[:, part, :] + jnp.concatenate(rows, axis=0)

    for turn in range(KMAX):
        for unit in range(LINES // 16):
            parts = [slice(16 * unit, 16 * unit + 8), slice(16 * unit + 8, 16 * unit + 16)]
            old = [(state_ref[:, part, :] if turn else shifted(part)).reshape(side, POINTS) for part in parts]
            high, low = halves(jnp.tanh(jnp.concatenate(old, axis=1)))
            change = dot(high_ref[...], high) + (dot(low_ref[...], high) + dot(high_ref[...], low))
            done = []
            for at, part in enumerate(parts):
                active = (counts_ref[part, :] > float(turn))[None]
                before = old[at].reshape(SPECIES, 8, POINTS)
                after = before + change[:, at * POINTS : (at + 1) * POINTS].reshape(SPECIES, 8, POINTS)
                done.append(jnp.where(active, after, before))
                state_ref[:, part, :] = done[at]
            if turn == KMAX - 1:
                finish(unit, done)


def pack_tables(owner_row, line_row, from_row, to_row, pick_ref, group_ref, placing_ref, aims_ref):
    lane = iota(1)
    pick_ref[...] = column(from_row).astype(jnp.int32) * SEG + lane % SEG
    landing = column(to_row)
    group_ref[...] = (lane // SEG - landing.astype(jnp.int32)) & 7
    owner = column(owner_row).astype(jnp.int32)
    earlier = (owner == owner_row) & (iota(0) < lane)
    rank = jnp.sum(earlier.astype(F32), axis=0, keepdims=True)
    aims_ref[...] = jnp.where(lane < 64, column(line_row) + 1.0, landing).astype(BF16)
    for slot in range(2):
        placing = ((iota(0) == owner_row) & (rank == slot)).astype(F32).astype(BF16)
        placing_ref[slot, :, :LINES] = placing
        placing_ref[slot, :, LINES:] = placing


def pack_segments(unit, values, pick_ref, group_ref, out_ref):
    parts = [slice(16 * unit, 16 * unit + 8), slice(16 * unit + 8, 16 * unit + 16)]
    for third in range(3):
        halves_of = []
        for part, value in zip(parts, values):
            pick, group = pick_ref[part, :], group_ref[part, :]
            gathered = lane_pick(value[8 * third], pick)
            for s in range(1, 8):
                gathered = jnp.where(group == s, lane_pick(value[8 * third + s], pick), gathered)
            halves_of.append(gathered)
        high, low = halves(jnp.concatenate(halves_of, axis=0))
        columns = slice(third * POINTS, (third + 1) * POINTS)
        out_ref[16 * unit : 16 * unit + 16, columns] = high
        out_ref[LINES + 16 * unit : LINES + 16 * unit + 16, columns] = low


def sending_rows(placing_ref, aims_ref, out_ref, send_ref):
    for slot in range(2):
        sending = dot(placing_ref[slot], out_ref[...])
        for third in range(3):
            send_ref[pl.ds(3 * slot + third, OWNERS, stride=ROWS), :] = sending[
                :, third * POINTS : (third + 1) * POINTS
            ]
        send_ref[pl.ds(6 + slot, OWNERS, stride=ROWS), :] = dot(placing_ref[slot, :, :LINES], aims_ref[...])


def splicing(received_ref, state_ref, write, parts_ref, hits_ref, gain_ref):
    place = iota(0).astype(F32)
    for slot in range(2):
        aim = jnp.transpose(received_ref[pl.ds(6 + slot, OWNERS, stride=ROWS), :])
        code = aim[64:65] * LINES + aim[:1] - 1.0
        rows = slice(slot * OWNERS, (slot + 1) * OWNERS)
        lows = slice((2 + slot) * OWNERS, (3 + slot) * OWNERS)
        for third in range(3):
            high, low = halves(received_ref[pl.ds(3 * slot + third, OWNERS, stride=ROWS), :])
            parts_ref[rows, third * POINTS : (third + 1) * POINTS] = high
            parts_ref[lows, third * POINTS : (third + 1) * POINTS] = low
        parts_ref[rows, 3 * POINTS :] = jnp.ones((OWNERS, POINTS), BF16)
        parts_ref[lows, 3 * POINTS :] = jnp.zeros((OWNERS, POINTS), BF16)
        for segment in range(8):
            hit = jnp.where(place + float(segment * LINES) == code, 0.5, 0.0).astype(BF16)
            hits_ref[segment * LINES : (segment + 1) * LINES, rows] = hit
            hits_ref[segment * LINES : (segment + 1) * LINES, lows] = hit
    gain_ref[...] = dot(hits_ref[...], parts_ref[...]).reshape(8, LINES, 4 * POINTS)
    group = iota(1, (8, POINTS)) // SEG
    bits = [(group & bit) != 0 for bit in (1, 2, 4)]

    def block(at, carry):
        first = pl.multiple_of(8 * at, 8)
        lines = pl.ds(first, 8)
        share = gain_ref[0, lines, 3 * POINTS :]
        for segment in range(1, 8):
            share = jnp.where(group == segment, gain_ref[segment, lines, 3 * POINTS :], share)
        keep = 1.0 - share
        for third in range(3):
            shifted = [gain_ref[segment, lines, third * POINTS : (third + 1) * POINTS] for segment in range(8)]
            for bit, mask in zip((1, 2, 4), bits):
                shifted = [jnp.where(mask, shifted[(i + bit) % 8], shifted[i]) for i in range(8)]
            for s in range(8):
                gained = shifted[-s % 8]
                if s:
                    gained = pltpu.roll(gained, POINTS - SEG * s, 1)
                write(8 * third + s, at, state_ref[8 * third + s, lines, :] * keep + gained)
        return carry

    lax.fori_loop(0, LINES // 8, block, 0, unroll=2)


def means_of(read):
    ones = jnp.full((8, 2 * POINTS), 1.0 / POINTS, BF16)
    rows = []
    for s in range(SPECIES):
        both = jnp.concatenate(halves(read(s)), axis=1)
        sums = lax.dot_general(ones, both, (((1,), (1,)), ((), ())), preferred_element_type=F32)
        rows.append(sums[:1])
    return jnp.concatenate(rows, axis=0)


def scales(diffusivity_row, eigen_row):
    row = jnp.concatenate([diffusivity_row, jnp.zeros((1, POINTS - SPECIES), F32)], axis=1)
    lane = iota(1, (SPECIES, POINTS))
    return jnp.where(lane == 0, 0.5, 1.0 / (1.0 + column(row)[:SPECIES] * eigen_row))


def first_mix_kernel(
    lines_hbm, start_hbm, diffusivity_hbm, eigen_hbm, first_hbm, second_hbm, rates_hbm, frozen_hbm,
    mixed_ref, high_ref, low_ref, scale_ref,
    lines_ref, start_ref, diffusivity_ref, eigen_ref, first_ref, second_ref, rates_ref, frozen_ref, index_ref, sems,
):
    here = [lines_ref.at[third].reshape(LINES, 8, POINTS) for third in range(3)]
    there = [lines_hbm.at[:, pl.ds(8 * third, 8), :] for third in range(3)]
    here = [rates_ref, frozen_ref, diffusivity_ref, eigen_ref, start_ref, first_ref, second_ref] + here
    there = [rates_hbm, frozen_hbm, diffusivity_hbm, eigen_hbm, start_hbm, first_hbm, second_hbm] + there
    copies = [pltpu.make_async_copy(a, b, sems.at[i]) for i, (a, b) in enumerate(zip(there, here))]
    for copy in copies:
        copy.start()
    for copy in copies[:7]:
        copy.wait()
    mix_tables(rates_ref[...], frozen_ref[...], high_ref, low_ref)
    scale_ref[...] = scales(diffusivity_ref[...], eigen_ref[...])

    def ready(third):
        copies[7 + third].wait()

    def read(s):
        return lines_ref[s // 8, pl.ds(s % 8, LINES, stride=8), :]

    mixing(read, start_ref[0, 0], scale_ref, first_ref, second_ref, mixed_ref, index_ref, ready)


def next_mix_kernel(state_ref, start_ref, scale_ref, first_ref, second_ref, mixed_ref, index_ref):
    mixing(lambda s: state_ref[s], start_ref[1, 0], scale_ref, first_ref, second_ref, mixed_ref, index_ref)


def react_kernel(
    step, mixed_ref, les_ref, grid_even_ref, grid_odd_ref, line_even_ref, line_odd_ref, owner_ref, line_ref, from_ref,
    to_ref, counts_ref, high_ref, low_ref, state_ref, send_ref, mid_ref, turns_ref, out_ref, pick_ref, group_ref,
    placing_ref, aims_ref,
):
    mid = middle(les_ref[:, 0], grid_even_ref[:, 0], grid_odd_ref[:, 0], line_even_ref[:, 0], line_odd_ref[:, 0])
    mid_ref[...] = mid
    rows = (ref[step, 0] for ref in (owner_ref, line_ref, from_ref, to_ref))
    pack_tables(*rows, pick_ref, group_ref, placing_ref, aims_ref)

    def finish(unit, values):
        pack_segments(unit, values, pick_ref, group_ref, out_ref)

    chemistry(counts_ref[0], turned(0.5 * mid), high_ref, low_ref, mixed_ref, state_ref, turns_ref, finish)
    sending_rows(placing_ref, aims_ref, out_ref, send_ref)


def next_splice_kernel(received_ref, state_ref, mid_ref, les_ref, lines_ref, parts_ref, hits_ref, gain_ref):
    def write(species, at, value):
        lines_ref[species, pl.ds(pl.multiple_of(8 * at, 8), 8), :] = value

    splicing(received_ref, state_ref, write, parts_ref, hits_ref, gain_ref)
    les_ref[:, 0] = 0.5 * mid_ref[...] + 0.5 * means_of(lambda s: lines_ref[s])


def last_splice_kernel(
    received_ref, state_ref, mid_ref, les_ref, lines_hbm, parts_ref, hits_ref, gain_ref, lines_ref, sems
):
    rows = 8 * SPECIES

    def out(at):
        part = pl.ds(pl.multiple_of(at * rows, rows), rows)
        return pltpu.make_async_copy(lines_ref.at[part], lines_hbm.at[part], sems.at[at])

    def write(species, at, value):
        lines_ref[pl.ds(at * rows + species, 8, stride=SPECIES), :] = value
        if species == SPECIES - 1:
            out(at).start()

    splicing(received_ref, state_ref, write, parts_ref, hits_ref, gain_ref)
    means = means_of(lambda s: lines_ref[pl.ds(s, LINES, stride=SPECIES), :])
    les_ref[:, 0] = 0.5 * mid_ref[...] + 0.5 * means
    for at in range(LINES // 8):
        out(at).wait()


VMEM = pl.BlockSpec(memory_space=pltpu.VMEM)
HBM = pl.BlockSpec(memory_space=pltpu.HBM)
STATE = jax.ShapeDtypeStruct((SPECIES, LINES, POINTS), F32)
FLAT = jax.ShapeDtypeStruct((LINES * SPECIES, POINTS), F32)
SPLICE_SCRATCH = [
    pltpu.VMEM((4 * OWNERS, 4 * POINTS), BF16),
    pltpu.VMEM((8 * LINES, 4 * OWNERS), BF16),
    pltpu.VMEM((8, LINES, 4 * POINTS), F32),
]


def call(kernel, inputs, outputs, scratch, micros, in_space=VMEM, out_specs=None):
    size = sum(x.size * x.dtype.itemsize for x in [*inputs, *outputs])
    if in_space is HBM:
        inputs = [pltpu.with_memory_space_constraint(x, pltpu.HBM) for x in inputs]
    return pl.pallas_call(
        kernel,
        out_shape=outputs,
        in_specs=[in_space] * len(inputs),
        out_specs=out_specs or [VMEM] * len(outputs),
        scratch_shapes=scratch,
        cost_estimate=pl.CostEstimate(flops=micros * 10**9, bytes_accessed=size, transcendentals=0),
        compiler_params=pltpu.CompilerParams(vmem_limit_bytes=32 << 20),
    )(*inputs)


def beside(field):
    around = []
    for axis in ("grid", "line"):
        peers = lax.axis_size(axis)
        for start in (0, 1):
            pairs = [(i, (i + 1) % peers) for i in range(start, peers, 2)]
            around.append(lax.ppermute(field, axis, pairs + [(b, a) for a, b in pairs]))
    return around


def body(
    les,
    lines,
    triplet_start,
    splice_owner,
    splice_line,
    splice_from,
    splice_to,
    chem_counts,
    diffusivity,
    rates,
    frozen_inverse,
):
    first_table, second_table, eigen = (jnp.asarray(x) for x in cosine_tables())
    side = SPECIES * 8
    send = jax.ShapeDtypeStruct((OWNERS * ROWS, POINTS), F32)
    plane = jax.ShapeDtypeStruct((SPECIES, LINES), F32)
    table = jax.ShapeDtypeStruct((side, side), BF16)
    owner = splice_owner.reshape(STEPS, 1, 1, LINES)
    field = les
    index = pltpu.VMEM((LINES, POINTS), jnp.int32)
    for step in range(STEPS):
        last = step == STEPS - 1
        rim = beside(field)
        if step == 0:
            inputs = [lines.reshape(LINES, SPECIES, POINTS), triplet_start, diffusivity.reshape(1, SPECIES), eigen]
            inputs += [first_table, second_table, rates, frozen_inverse]
            scratch = [pltpu.VMEM((3, LINES * 8, POINTS), F32)] + [pltpu.VMEM(x.shape, x.dtype) for x in inputs[1:]]
            scratch += [index, pltpu.SemaphoreType.DMA((len(inputs) + 2,))]
            mixed, high, low, scale = call(
                first_mix_kernel, inputs, [STATE, table, table, plane], scratch, 4, in_space=HBM
            )
        else:
            inputs = [state, triplet_start, scale, first_table, second_table]
            (mixed,) = call(next_mix_kernel, inputs, [STATE], [index], 3)

        def react(*refs, step=step):
            react_kernel(step, *refs)

        inputs = [mixed, field, *rim, owner, splice_line, splice_from, splice_to, chem_counts, high, low]
        scratch = [
            pltpu.VMEM((LINES, POINTS), F32),
            pltpu.VMEM((2 * LINES, 3 * POINTS), BF16),
            index,
            index,
            pltpu.VMEM((2, OWNERS, 2 * LINES), BF16),
            pltpu.VMEM((LINES, POINTS), BF16),
        ]
        state, sending, mid = call(react, inputs, [STATE, send, plane], scratch, 8)
        received = lax.all_to_all(
            sending.reshape(OWNERS, ROWS, POINTS), ("grid", "line"), split_axis=0, concat_axis=0, tiled=True
        ).reshape(OWNERS * ROWS, POINTS)
        inputs = [received, state, mid]
        outputs = [jax.ShapeDtypeStruct(les.shape, F32), FLAT if last else STATE]
        if last:
            scratch = SPLICE_SCRATCH + [pltpu.VMEM(FLAT.shape, F32), pltpu.SemaphoreType.DMA((LINES // 8,))]
            field, state = call(last_splice_kernel, inputs, outputs, scratch, 3, out_specs=[VMEM, HBM])
        else:
            field, state = call(next_splice_kernel, inputs, outputs, SPLICE_SCRATCH, 3)
    return (field, state.reshape(lines.shape))


def solution(mesh):
    in_specs = (
        P(None, "grid", "line"),
        P("grid", "line", None, None, None),
        P(None, "grid", "line", None),
        P(None, "grid", "line", None, None),
        P(None, "grid", "line", None),
        P(None, "grid", "line", None),
        P(None, "grid", "line", None),
        P("grid", "line", None),
        P(),
        P(),
        P(),
    )
    out_specs = (P(None, "grid", "line"), P("grid", "line", None, None, None))
    return jax.shard_map(body, mesh=mesh, in_specs=in_specs, out_specs=out_specs, check_vma=False)
```

```python
import jax
import jax.numpy as jnp
import numpy as np
from jax import lax
from jax.experimental import pallas as pl
from jax.experimental.pallas import tpu as pltpu
from jax.sharding import PartitionSpec as P

SEG = 16
TRIP = 48
KMAX = 6
STEPS = 2
LES_RATE = 0.2
SPECIES = 24
POINTS = 128
LINES = 128
OWNERS = 128
ROWS = 6
AIMS = 1
F32 = jnp.float32
BF16 = jnp.bfloat16


def cosine_tables():
    k = np.arange(POINTS)[:, None]
    p = np.arange(POINTS)[None, :]
    basis = np.sqrt(2.0 / POINTS) * np.cos(np.pi * k * (2 * p + 1) / (2 * POINTS))
    basis[0] = 1.0 / np.sqrt(POINTS)
    tables = []
    for table in (basis.T, basis):
        high = table.astype(BF16)
        low = (table - high.astype(np.float64)).astype(BF16)
        half = np.concatenate([high, low], axis=1)
        tables.append(np.concatenate([half, half], axis=0))
    eigen = 4.0 * np.sin(np.pi * np.arange(POINTS) / (2 * POINTS)) ** 2
    return tables[0], tables[1], eigen.astype(np.float32)[None, :]


def halves(value):
    high = value.astype(BF16)
    return high, (value - high.astype(F32)).astype(BF16)


def dot(a, b):
    return jnp.dot(a, b, preferred_element_type=F32)


def iota(axis, shape=(LINES, POINTS)):
    return lax.broadcasted_iota(jnp.int32, shape, axis)


def column(row):
    return jnp.transpose(jnp.broadcast_to(row.astype(F32), (LINES, POINTS)))


def lane_pick(value, index):
    return jnp.take_along_axis(value, index, axis=1, mode="promise_in_bounds")


def mix_tables(rates, frozen, high_ref, low_ref):
    exact = dict(precision=lax.Precision.HIGHEST, preferred_element_type=F32)
    matrix = jnp.dot(frozen, rates, **exact)
    side = SPECIES * 8
    spread = (iota(0, (side, SPECIES)) // 8 == iota(1, (side, SPECIES))).astype(F32)
    gather = (iota(0, (SPECIES, side)) == iota(1, (SPECIES, side)) // 8).astype(F32)
    wide = jnp.dot(jnp.dot(spread, matrix, **exact), gather, **exact)
    same = iota(0, (side, side)) % 8 == iota(1, (side, side)) % 8
    high, low = halves(jnp.where(same, wide, 0.0))
    high_ref[...] = high
    low_ref[...] = low


def middle(les, grid_even, grid_odd, line_even, line_odd):
    row, place = lax.axis_index("grid"), lax.axis_index("line")
    inner = jnp.logical_and(row > 0, row < lax.axis_size("grid") - 1)
    even = place % 2 == 0
    west = jnp.where(even, line_odd, line_even)
    east = jnp.where(even, line_even, line_odd)
    west = jnp.where(place > 0, west, 0.0)
    east = jnp.where(place < lax.axis_size("line") - 1, east, 0.0)
    lane = iota(1, (SPECIES, LINES))
    left = jnp.where(lane == 0, pltpu.roll(west, 1, 1), pltpu.roll(les, 1, 1))
    right = jnp.where(lane == LINES - 1, pltpu.roll(east, LINES - 1, 1), pltpu.roll(les, LINES - 1, 1))
    return les + LES_RATE * (grid_even + jnp.where(inner, grid_odd, 0.0) + left + right - 4.0 * les)


def turned(value):
    pad = jnp.zeros((POINTS - SPECIES, LINES), F32)
    return jnp.transpose(jnp.concatenate([value, pad], axis=0))


def triplet_index(start):
    place = iota(1)
    start = start.astype(jnp.int32)
    rel = place - start
    third = TRIP // 3
    source = jnp.where(
        rel < third,
        3 * rel,
        jnp.where(rel < 2 * third, 3 * (2 * third - 1 - rel) + 1, 3 * (rel - 2 * third) + 2),
    )
    return jnp.where((rel >= 0) & (rel < TRIP), source + start, place)


def mixing(read, start_row, scale_ref, first_ref, second_ref, state_ref, index_ref):
    index_ref[...] = triplet_index(column(start_row))
    group = 8

    for at in range(SPECIES // group):
        species = [at * group + i for i in range(group)]
        value = jnp.concatenate([lane_pick(read(s), index_ref[...]) for s in species], axis=0)
        wide = dot(jnp.concatenate(halves(value), axis=1), first_ref[...])
        value = wide[:, :POINTS] + wide[:, POINTS:]
        value = value.reshape(group, LINES, POINTS)
        value = jnp.concatenate([value[i] * scale_ref[s : s + 1, :] for i, s in enumerate(species)], axis=0)
        wide = dot(jnp.concatenate(halves(value), axis=1), second_ref[...])
        value = (wide[:, :POINTS] + wide[:, POINTS:]).reshape(group, LINES, POINTS)
        for i, s in enumerate(species):
            state_ref[s] = value[i]


def chemistry(turns_ref, shift, high_ref, low_ref, mixed_ref, state_ref, finish):
    side = SPECIES * 8

    def shifted(part):
        rows = [jnp.broadcast_to(shift[part, s : s + 1], (8, POINTS))[None] for s in range(SPECIES)]
        return mixed_ref[:, part, :] + jnp.concatenate(rows, axis=0)

    for turn in range(KMAX):
        for unit in range(LINES // 16):
            parts = [slice(16 * unit, 16 * unit + 8), slice(16 * unit + 8, 16 * unit + 16)]
            old = [(state_ref[:, part, :] if turn else shifted(part)).reshape(side, POINTS) for part in parts]
            high, low = halves(jnp.tanh(jnp.concatenate(old, axis=1)))
            change = dot(high_ref[...], high) + (dot(low_ref[...], high) + dot(high_ref[...], low))
            done = []
            for at, part in enumerate(parts):
                active = (turns_ref[part, :] > float(turn))[None]
                before = old[at].reshape(SPECIES, 8, POINTS)
                after = before + change[:, at * POINTS : (at + 1) * POINTS].reshape(SPECIES, 8, POINTS)
                done.append(jnp.where(active, after, before))
                state_ref[:, part, :] = done[at]
            if turn == KMAX - 1:
                finish(unit, done)


def pick_tables(from_row, to_row, pick_ref, group_ref):
    lane = iota(1)
    pick_ref[...] = column(from_row).astype(jnp.int32) * SEG + lane % SEG
    group_ref[...] = (lane // SEG - column(to_row).astype(jnp.int32)) & 7


def place_tables(owner_row, placing_ref):
    lane = iota(1)
    owner = column(owner_row).astype(jnp.int32)
    earlier = (owner == owner_row) & (iota(0) < lane)
    rank = jnp.sum(earlier.astype(F32), axis=0, keepdims=True)
    for slot in range(2):
        placing = ((iota(0) == owner_row) & (rank == slot)).astype(F32).astype(BF16)
        placing_ref[slot, :, :LINES] = placing
        placing_ref[slot, :, LINES:] = placing


def aim_rows(step, line_row, to_row):
    lane = iota(1)
    line, segment = column(line_row) + 1.0, column(to_row)
    rows = []
    for slot in range(2):
        at = 4 * step + 2 * slot
        rows.append(jnp.where(lane // SEG == at, line, jnp.where(lane // SEG == at + 1, segment, 0.0)).astype(BF16))
    return rows


def aim_codes(aims):
    turned_aims = jnp.transpose(aims)

    def code(at):
        line, segment = turned_aims[SEG * at : SEG * at + 1], turned_aims[SEG * at + SEG : SEG * at + SEG + 1]
        return segment * LINES + line - 1.0

    return [[code(4 * step + 2 * slot) for slot in range(2)] for step in range(STEPS)]


def hit_table(codes, hits_ref):
    place = iota(0).astype(F32)
    for slot in range(2):
        for segment in range(8):
            hit = jnp.where(place + float(segment * LINES) == codes[slot], 0.5, 0.0).astype(BF16)
            for at in (slot, 2 + slot):
                hits_ref[segment * LINES : (segment + 1) * LINES, at * OWNERS : (at + 1) * OWNERS] = hit


def pack_segments(unit, values, pick_ref, group_ref, out_ref):
    parts = [slice(16 * unit, 16 * unit + 8), slice(16 * unit + 8, 16 * unit + 16)]
    for third in range(3):
        halves_of = []
        for part, value in zip(parts, values):
            pick, group = pick_ref[part, :], group_ref[part, :]
            gathered = lane_pick(value[8 * third], pick)
            for s in range(1, 8):
                gathered = jnp.where(group == s, lane_pick(value[8 * third + s], pick), gathered)
            halves_of.append(gathered)
        high, low = halves(jnp.concatenate(halves_of, axis=0))
        columns = slice(third * POINTS, (third + 1) * POINTS)
        out_ref[16 * unit : 16 * unit + 16, columns] = high
        out_ref[LINES + 16 * unit : LINES + 16 * unit + 16, columns] = low


def sending_rows(placing_ref, out_ref, send_ref, rows):
    for slot in range(2):
        sending = dot(placing_ref[slot], out_ref[...])
        for third in range(3):
            send_ref[pl.ds(3 * slot + third, OWNERS, stride=rows), :] = sending[
                :, third * POINTS : (third + 1) * POINTS
            ]


def splicing(received_ref, rows, state_ref, write, parts_ref, hits_ref, gain_ref):
    for slot in range(2):
        highs = slice(slot * OWNERS, (slot + 1) * OWNERS)
        lows = slice((2 + slot) * OWNERS, (3 + slot) * OWNERS)
        for third in range(3):
            high, low = halves(received_ref[pl.ds(3 * slot + third, OWNERS, stride=rows), :])
            parts_ref[highs, third * POINTS : (third + 1) * POINTS] = high
            parts_ref[lows, third * POINTS : (third + 1) * POINTS] = low
        parts_ref[highs, 3 * POINTS :] = jnp.ones((OWNERS, POINTS), BF16)
        parts_ref[lows, 3 * POINTS :] = jnp.zeros((OWNERS, POINTS), BF16)
    gain_ref[...] = dot(hits_ref[...], parts_ref[...]).reshape(8, LINES, 4 * POINTS)
    group = iota(1, (8, POINTS)) // SEG
    bits = [(group & bit) != 0 for bit in (1, 2, 4)]

    def block(at, carry):
        first = pl.multiple_of(8 * at, 8)
        lines = pl.ds(first, 8)
        share = gain_ref[0, lines, 3 * POINTS :]
        for segment in range(1, 8):
            share = jnp.where(group == segment, gain_ref[segment, lines, 3 * POINTS :], share)
        keep = 1.0 - share
        for third in range(3):
            shifted = [gain_ref[segment, lines, third * POINTS : (third + 1) * POINTS] for segment in range(8)]
            for bit, mask in zip((1, 2, 4), bits):
                shifted = [jnp.where(mask, shifted[(i + bit) % 8], shifted[i]) for i in range(8)]
            for s in range(8):
                gained = shifted[-s % 8]
                if s:
                    gained = pltpu.roll(gained, POINTS - SEG * s, 1)
                write(8 * third + s, at, state_ref[8 * third + s, lines, :] * keep + gained)
        return carry

    lax.fori_loop(0, LINES // 8, block, 0, unroll=2)


def means_of(read):
    ones = jnp.full((8, 2 * POINTS), 1.0 / POINTS, BF16)
    rows = []
    for s in range(SPECIES):
        both = jnp.concatenate(halves(read(s)), axis=1)
        sums = lax.dot_general(ones, both, (((1,), (1,)), ((), ())), preferred_element_type=F32)
        rows.append(sums[:1])
    return jnp.concatenate(rows, axis=0)


def scales(diffusivity_row, eigen_row):
    row = jnp.concatenate([diffusivity_row, jnp.zeros((1, POINTS - SPECIES), F32)], axis=1)
    lane = iota(1, (SPECIES, POINTS))
    return jnp.where(lane == 0, 0.5, 1.0 / (1.0 + column(row)[:SPECIES] * eigen_row))


def first_mix_kernel(
    lines_hbm, start_hbm, diffusivity_hbm, eigen_hbm, first_hbm, second_hbm, rates_hbm, frozen_hbm,
    mixed_ref, high_ref, low_ref, scale_ref,
    lines_ref, start_ref, diffusivity_ref, eigen_ref, first_ref, second_ref, rates_ref, frozen_ref, index_ref, sems,
):
    here = [lines_ref.at[third].reshape(LINES, 8, POINTS) for third in range(3)]
    there = [lines_hbm.at[:, pl.ds(8 * third, 8), :] for third in range(3)]
    here = [rates_ref, frozen_ref, diffusivity_ref, eigen_ref, start_ref, first_ref, second_ref] + here
    there = [rates_hbm, frozen_hbm, diffusivity_hbm, eigen_hbm, start_hbm, first_hbm, second_hbm] + there
    copies = [pltpu.make_async_copy(a, b, sems.at[i]) for i, (a, b) in enumerate(zip(there, here))]
    for copy in copies:
        copy.start()
    for copy in copies:
        copy.wait()
    mix_tables(rates_ref[...], frozen_ref[...], high_ref, low_ref)
    scale_ref[...] = scales(diffusivity_ref[...], eigen_ref[...])

    def read(s):
        return lines_ref[s // 8, pl.ds(s % 8, LINES, stride=8), :]

    mixing(read, start_ref[0, 0], scale_ref, first_ref, second_ref, mixed_ref, index_ref)


def next_mix_kernel(
    state_ref, start_ref, scale_ref, first_ref, second_ref, from_ref, to_ref, codes_ref,
    mixed_ref, pick_ref, group_ref, hits_ref, index_ref,
):
    mixing(lambda s: state_ref[s], start_ref[1, 0], scale_ref, first_ref, second_ref, mixed_ref, index_ref)
    pick_tables(from_ref[1, 0], to_ref[1, 0], pick_ref, group_ref)
    hit_table([codes_ref[:1], codes_ref[1:2]], hits_ref)


def react(mixed_ref, les_ref, rim_refs, turns_ref, high_ref, low_ref, pick_ref, group_ref, state_ref, mid_ref, out_ref):
    mid = middle(les_ref[:, 0], *[ref[:, 0] for ref in rim_refs])
    mid_ref[...] = mid

    def finish(unit, values):
        pack_segments(unit, values, pick_ref, group_ref, out_ref)

    chemistry(turns_ref, turned(0.5 * mid), high_ref, low_ref, mixed_ref, state_ref, finish)


def first_react_kernel(
    mixed_ref, les_ref, grid_even_ref, grid_odd_ref, line_even_ref, line_odd_ref, high_ref, low_ref, owner_ref, line_ref,
    from_ref, to_ref, counts_ref, state_ref, send_ref, mid_ref, turns_ref, later_ref, out_ref, pick_ref, group_ref,
    placing_ref,
):
    turns_ref[...] = column(counts_ref[0])
    pick_tables(from_ref[0, 0], to_ref[0, 0], pick_ref, group_ref)
    place_tables(owner_ref[0, 0], placing_ref)
    place_tables(owner_ref[1, 0], later_ref)
    aims = [row for step in range(STEPS) for row in aim_rows(step, line_ref[step, 0], to_ref[step, 0])]
    placings = [ref[slot, :, :LINES] for ref in (placing_ref, later_ref) for slot in range(2)]
    rows = ROWS + AIMS
    send_ref[pl.ds(ROWS, OWNERS, stride=rows), :] = dot(
        jnp.concatenate(placings, axis=1), jnp.concatenate(aims, axis=0)
    )
    rim = (grid_even_ref, grid_odd_ref, line_even_ref, line_odd_ref)
    react(mixed_ref, les_ref, rim, turns_ref, high_ref, low_ref, pick_ref, group_ref, state_ref, mid_ref, out_ref)
    sending_rows(placing_ref, out_ref, send_ref, rows)


def next_react_kernel(
    mixed_ref, les_ref, grid_even_ref, grid_odd_ref, line_even_ref, line_odd_ref, high_ref, low_ref, pick_ref, group_ref,
    turns_ref, placing_ref, state_ref, send_ref, mid_ref, out_ref,
):
    rim = (grid_even_ref, grid_odd_ref, line_even_ref, line_odd_ref)
    react(mixed_ref, les_ref, rim, turns_ref, high_ref, low_ref, pick_ref, group_ref, state_ref, mid_ref, out_ref)
    sending_rows(placing_ref, out_ref, send_ref, ROWS)


def next_splice_kernel(received_ref, state_ref, mid_ref, les_ref, lines_ref, codes_ref, parts_ref, gain_ref, hits_ref):
    def write(species, at, value):
        lines_ref[species, pl.ds(pl.multiple_of(8 * at, 8), 8), :] = value

    rows = ROWS + AIMS
    codes = aim_codes(received_ref[pl.ds(ROWS, OWNERS, stride=rows), :])
    codes_ref[...] = jnp.concatenate(codes[1] + [jnp.zeros((6, OWNERS), F32)], axis=0)
    hit_table(codes[0], hits_ref)
    splicing(received_ref, rows, state_ref, write, parts_ref, hits_ref, gain_ref)
    les_ref[:, 0] = 0.5 * mid_ref[...] + 0.5 * means_of(lambda s: lines_ref[s])


def last_splice_kernel(
    received_ref, state_ref, mid_ref, hits_ref, les_ref, lines_hbm, parts_ref, gain_ref, lines_ref, sems
):
    rows = 8 * SPECIES

    def out(at):
        part = pl.ds(pl.multiple_of(at * rows, rows), rows)
        return pltpu.make_async_copy(lines_ref.at[part], lines_hbm.at[part], sems.at[at])

    def write(species, at, value):
        lines_ref[pl.ds(at * rows + species, 8, stride=SPECIES), :] = value
        if species == SPECIES - 1:
            out(at).start()

    splicing(received_ref, ROWS, state_ref, write, parts_ref, hits_ref, gain_ref)
    means = means_of(lambda s: lines_ref[pl.ds(s, LINES, stride=SPECIES), :])
    les_ref[:, 0] = 0.5 * mid_ref[...] + 0.5 * means
    for at in range(LINES // 8):
        out(at).wait()


VMEM = pl.BlockSpec(memory_space=pltpu.VMEM)
HBM = pl.BlockSpec(memory_space=pltpu.HBM)
STATE = jax.ShapeDtypeStruct((SPECIES, LINES, POINTS), F32)
FLAT = jax.ShapeDtypeStruct((LINES * SPECIES, POINTS), F32)
SPLICE_SCRATCH = [pltpu.VMEM((4 * OWNERS, 4 * POINTS), BF16), pltpu.VMEM((8, LINES, 4 * POINTS), F32)]


def call(kernel, inputs, outputs, scratch, micros, in_space=VMEM, out_specs=None):
    size = sum(x.size * x.dtype.itemsize for x in [*inputs, *outputs])
    if in_space is HBM:
        inputs = [pltpu.with_memory_space_constraint(x, pltpu.HBM) for x in inputs]
    return pl.pallas_call(
        kernel,
        out_shape=outputs,
        in_specs=[in_space] * len(inputs),
        out_specs=out_specs or [VMEM] * len(outputs),
        scratch_shapes=scratch,
        cost_estimate=pl.CostEstimate(flops=micros * 10**9, bytes_accessed=size, transcendentals=0),
        compiler_params=pltpu.CompilerParams(vmem_limit_bytes=32 << 20),
    )(*inputs)


def beside(field):
    around = []
    for axis in ("grid", "line"):
        peers = lax.axis_size(axis)
        for start in (0, 1):
            pairs = [(i, (i + 1) % peers) for i in range(start, peers, 2)]
            around.append(lax.ppermute(field, axis, pairs + [(b, a) for a, b in pairs]))
    return around


def body(
    les,
    lines,
    triplet_start,
    splice_owner,
    splice_line,
    splice_from,
    splice_to,
    chem_counts,
    diffusivity,
    rates,
    frozen_inverse,
):
    def shaped(shape, dtype=F32):
        return jax.ShapeDtypeStruct(shape, dtype)

    first_table, second_table, eigen = (jnp.asarray(x) for x in cosine_tables())
    side = SPECIES * 8
    plane = shaped((SPECIES, LINES))
    owner = splice_owner.reshape(STEPS, 1, 1, LINES)
    square = shaped((LINES, POINTS))
    index = shaped((LINES, POINTS), jnp.int32)
    placing = shaped((2, OWNERS, 2 * LINES), BF16)
    hits = shaped((8 * LINES, 4 * OWNERS), BF16)
    scratch_of = lambda x: pltpu.VMEM(x.shape, x.dtype)
    outgoing = pltpu.VMEM((2 * LINES, 3 * POINTS), BF16)

    def exchange(sending):
        sending = sending.reshape(OWNERS, 1, -1)
        received = lax.all_to_all(sending, ("grid", "line"), split_axis=0, concat_axis=0, tiled=True)
        return received.reshape(-1, POINTS)

    rim = beside(les)
    inputs = [lines.reshape(LINES, SPECIES, POINTS), triplet_start, diffusivity.reshape(1, SPECIES), eigen]
    inputs += [first_table, second_table, rates, frozen_inverse]
    scratch = [pltpu.VMEM((3, LINES * 8, POINTS), F32)] + [scratch_of(x) for x in inputs[1:]]
    scratch += [scratch_of(index), pltpu.SemaphoreType.DMA((len(inputs) + 2,))]
    table = shaped((side, side), BF16)
    mixed, high, low, scale = call(first_mix_kernel, inputs, [STATE, table, table, plane], scratch, 4, in_space=HBM)

    inputs = [mixed, les, *rim, high, low, owner, splice_line, splice_from, splice_to, chem_counts]
    outputs = [STATE, shaped((OWNERS * (ROWS + AIMS), POINTS)), plane, square, placing]
    scratch = [outgoing, scratch_of(index), scratch_of(index), scratch_of(placing)]
    state, sending, mid, turns, later = call(first_react_kernel, inputs, outputs, scratch, 6)

    inputs = [exchange(sending), state, mid]
    outputs = [shaped(les.shape), STATE, shaped((8, OWNERS))]
    field, state, codes = call(next_splice_kernel, inputs, outputs, SPLICE_SCRATCH + [scratch_of(hits)], 3)

    rim = beside(field)
    inputs = [state, triplet_start, scale, first_table, second_table, splice_from, splice_to, codes]
    mixed, pick, group, landing = call(
        next_mix_kernel, inputs, [STATE, index, index, hits], [scratch_of(index)], 3
    )

    inputs = [mixed, field, *rim, high, low, pick, group, turns, later]
    outputs = [STATE, shaped((OWNERS * ROWS, POINTS)), plane]
    state, sending, mid = call(next_react_kernel, inputs, outputs, [outgoing], 6)

    inputs = [exchange(sending), state, mid, landing]
    outputs = [shaped(les.shape), FLAT]
    scratch = SPLICE_SCRATCH + [scratch_of(FLAT), pltpu.SemaphoreType.DMA((LINES // 8,))]
    field, state = call(last_splice_kernel, inputs, outputs, scratch, 3, out_specs=[VMEM, HBM])
    return (field, state.reshape(lines.shape))


def solution(mesh):
    in_specs = (
        P(None, "grid", "line"),
        P("grid", "line", None, None, None),
        P(None, "grid", "line", None),
        P(None, "grid", "line", None, None),
        P(None, "grid", "line", None),
        P(None, "grid", "line", None),
        P(None, "grid", "line", None),
        P("grid", "line", None),
        P(),
        P(),
        P(),
    )
    out_specs = (P(None, "grid", "line"), P("grid", "line", None, None, None))
    return jax.shard_map(body, mesh=mesh, in_specs=in_specs, out_specs=out_specs, check_vma=False)
```

```python
import jax
import jax.numpy as jnp
import numpy as np
from jax import lax
from jax.experimental import pallas as pl
from jax.experimental.pallas import tpu as pltpu
from jax.sharding import PartitionSpec as P

SEG = 16
TRIP = 48
KMAX = 6
STEPS = 2
LES_RATE = 0.2
SPECIES = 24
POINTS = 128
LINES = 128
OWNERS = 128
ROWS = 6
AIMS = 1
F32 = jnp.float32
BF16 = jnp.bfloat16


def cosine_tables():
    k = np.arange(POINTS)[:, None]
    p = np.arange(POINTS)[None, :]
    basis = np.sqrt(2.0 / POINTS) * np.cos(np.pi * k * (2 * p + 1) / (2 * POINTS))
    basis[0] = 1.0 / np.sqrt(POINTS)
    tables = []
    for table in (basis.T, basis):
        high = table.astype(BF16)
        low = (table - high.astype(np.float64)).astype(BF16)
        half = np.concatenate([high, low], axis=1)
        tables.append(np.concatenate([half, half], axis=0))
    eigen = 4.0 * np.sin(np.pi * np.arange(POINTS) / (2 * POINTS)) ** 2
    return tables[0], tables[1], eigen.astype(np.float32)[None, :]


def halves(value):
    high = value.astype(BF16)
    return high, (value - high.astype(F32)).astype(BF16)


def dot(a, b):
    return jnp.dot(a, b, preferred_element_type=F32)


def iota(axis, shape=(LINES, POINTS)):
    return lax.broadcasted_iota(jnp.int32, shape, axis)


def column(row):
    return jnp.transpose(jnp.broadcast_to(row.astype(F32), (LINES, POINTS)))


def lane_pick(value, index):
    return jnp.take_along_axis(value, index, axis=1, mode="promise_in_bounds")


def mix_tables(rates, frozen, high_ref, low_ref):
    exact = dict(precision=lax.Precision.HIGHEST, preferred_element_type=F32)
    matrix = jnp.dot(frozen, rates, **exact)
    side = SPECIES * 8
    spread = (iota(0, (side, SPECIES)) // 8 == iota(1, (side, SPECIES))).astype(F32)
    gather = (iota(0, (SPECIES, side)) == iota(1, (SPECIES, side)) // 8).astype(F32)
    wide = jnp.dot(jnp.dot(spread, matrix, **exact), gather, **exact)
    same = iota(0, (side, side)) % 8 == iota(1, (side, side)) % 8
    high, low = halves(jnp.where(same, wide, 0.0))
    high_ref[...] = high
    low_ref[...] = low


def middle(les, grid_even, grid_odd, line_even, line_odd):
    row, place = lax.axis_index("grid"), lax.axis_index("line")
    inner = jnp.logical_and(row > 0, row < lax.axis_size("grid") - 1)
    even = place % 2 == 0
    west = jnp.where(even, line_odd, line_even)
    east = jnp.where(even, line_even, line_odd)
    west = jnp.where(place > 0, west, 0.0)
    east = jnp.where(place < lax.axis_size("line") - 1, east, 0.0)
    lane = iota(1, (SPECIES, LINES))
    left = jnp.where(lane == 0, pltpu.roll(west, 1, 1), pltpu.roll(les, 1, 1))
    right = jnp.where(lane == LINES - 1, pltpu.roll(east, LINES - 1, 1), pltpu.roll(les, LINES - 1, 1))
    return les + LES_RATE * (grid_even + jnp.where(inner, grid_odd, 0.0) + left + right - 4.0 * les)


def turned(value):
    pad = jnp.zeros((POINTS - SPECIES, LINES), F32)
    return jnp.transpose(jnp.concatenate([value, pad], axis=0))


def triplet_index(start):
    place = iota(1)
    start = start.astype(jnp.int32)
    rel = place - start
    third = TRIP // 3
    source = jnp.where(
        rel < third,
        3 * rel,
        jnp.where(rel < 2 * third, 3 * (2 * third - 1 - rel) + 1, 3 * (rel - 2 * third) + 2),
    )
    return jnp.where((rel >= 0) & (rel < TRIP), source + start, place)


def mixing(read, start_row, scale_ref, first_ref, second_ref, state_ref, index_ref):
    index_ref[...] = triplet_index(column(start_row))
    group = 8

    for at in range(SPECIES // group):
        species = [at * group + i for i in range(group)]
        value = jnp.concatenate([lane_pick(read(s), index_ref[...]) for s in species], axis=0)
        wide = dot(jnp.concatenate(halves(value), axis=1), first_ref[...])
        value = wide[:, :POINTS] + wide[:, POINTS:]
        value = value.reshape(group, LINES, POINTS)
        value = jnp.concatenate([value[i] * scale_ref[s : s + 1, :] for i, s in enumerate(species)], axis=0)
        wide = dot(jnp.concatenate(halves(value), axis=1), second_ref[...])
        value = (wide[:, :POINTS] + wide[:, POINTS:]).reshape(group, LINES, POINTS)
        for i, s in enumerate(species):
            state_ref[s] = value[i]


def chemistry(turns_ref, shift, high_ref, low_ref, mixed_ref, state_ref, finish):
    side = SPECIES * 8

    def shifted(part):
        rows = [jnp.broadcast_to(shift[part, s : s + 1], (8, POINTS))[None] for s in range(SPECIES)]
        return mixed_ref[:, part, :] + jnp.concatenate(rows, axis=0)

    for turn in range(KMAX):
        for unit in range(LINES // 16):
            parts = [slice(16 * unit, 16 * unit + 8), slice(16 * unit + 8, 16 * unit + 16)]
            old = [(state_ref[:, part, :] if turn else shifted(part)).reshape(side, POINTS) for part in parts]
            high, low = halves(jnp.tanh(jnp.concatenate(old, axis=1)))
            change = dot(high_ref[...], high) + (dot(low_ref[...], high) + dot(high_ref[...], low))
            done = []
            for at, part in enumerate(parts):
                active = (turns_ref[part, :] > float(turn))[None]
                before = old[at].reshape(SPECIES, 8, POINTS)
                after = before + change[:, at * POINTS : (at + 1) * POINTS].reshape(SPECIES, 8, POINTS)
                done.append(jnp.where(active, after, before))
                state_ref[:, part, :] = done[at]
            if turn == KMAX - 1:
                finish(unit, done)


def pick_tables(from_row, to_row, pick_ref, group_ref):
    lane = iota(1)
    pick_ref[...] = column(from_row).astype(jnp.int32) * SEG + lane % SEG
    group_ref[...] = (lane // SEG - column(to_row).astype(jnp.int32)) & 7


def place_tables(owner_row, placing_ref):
    lane = iota(1)
    owner = column(owner_row).astype(jnp.int32)
    earlier = (owner == owner_row) & (iota(0) < lane)
    rank = jnp.sum(earlier.astype(F32), axis=0, keepdims=True)
    for slot in range(2):
        placing = ((iota(0) == owner_row) & (rank == slot)).astype(F32).astype(BF16)
        placing_ref[slot, :, :LINES] = placing
        placing_ref[slot, :, LINES:] = placing


def aim_rows(step, line_row, to_row):
    lane = iota(1)
    line, segment = column(line_row) + 1.0, column(to_row)
    rows = []
    for slot in range(2):
        at = 4 * step + 2 * slot
        rows.append(jnp.where(lane // SEG == at, line, jnp.where(lane // SEG == at + 1, segment, 0.0)).astype(BF16))
    return rows


def aim_codes(aims):
    turned_aims = jnp.transpose(aims)

    def code(at):
        line, segment = turned_aims[SEG * at : SEG * at + 1], turned_aims[SEG * at + SEG : SEG * at + SEG + 1]
        return segment * LINES + line - 1.0

    return [[code(4 * step + 2 * slot) for slot in range(2)] for step in range(STEPS)]


def hit_table(codes, hits_ref):
    place = iota(0).astype(F32)
    for slot in range(2):
        for segment in range(8):
            hit = jnp.where(place + float(segment * LINES) == codes[slot], 0.5, 0.0).astype(BF16)
            for at in (slot, 2 + slot):
                hits_ref[segment * LINES : (segment + 1) * LINES, at * OWNERS : (at + 1) * OWNERS] = hit


def pack_segments(unit, values, pick_ref, group_ref, out_ref):
    parts = [slice(16 * unit, 16 * unit + 8), slice(16 * unit + 8, 16 * unit + 16)]
    for third in range(3):
        halves_of = []
        for part, value in zip(parts, values):
            pick, group = pick_ref[part, :], group_ref[part, :]
            gathered = lane_pick(value[8 * third], pick)
            for s in range(1, 8):
                gathered = jnp.where(group == s, lane_pick(value[8 * third + s], pick), gathered)
            halves_of.append(gathered)
        high, low = halves(jnp.concatenate(halves_of, axis=0))
        columns = slice(third * POINTS, (third + 1) * POINTS)
        out_ref[16 * unit : 16 * unit + 16, columns] = high
        out_ref[LINES + 16 * unit : LINES + 16 * unit + 16, columns] = low


def sending_rows(placing_ref, out_ref, send_ref, rows):
    for slot in range(2):
        sending = dot(placing_ref[slot], out_ref[...])
        for third in range(3):
            send_ref[pl.ds(3 * slot + third, OWNERS, stride=rows), :] = sending[
                :, third * POINTS : (third + 1) * POINTS
            ]


def splicing(received_ref, rows, state_ref, write, parts_ref, hits_ref, gain_ref):
    for slot in range(2):
        highs = slice(slot * OWNERS, (slot + 1) * OWNERS)
        lows = slice((2 + slot) * OWNERS, (3 + slot) * OWNERS)
        for third in range(3):
            high, low = halves(received_ref[pl.ds(3 * slot + third, OWNERS, stride=rows), :])
            parts_ref[highs, third * POINTS : (third + 1) * POINTS] = high
            parts_ref[lows, third * POINTS : (third + 1) * POINTS] = low
        parts_ref[highs, 3 * POINTS :] = jnp.ones((OWNERS, POINTS), BF16)
        parts_ref[lows, 3 * POINTS :] = jnp.zeros((OWNERS, POINTS), BF16)
    gain_ref[...] = dot(hits_ref[...], parts_ref[...]).reshape(8, LINES, 4 * POINTS)
    group = iota(1, (8, POINTS)) // SEG
    bits = [(group & bit) != 0 for bit in (1, 2, 4)]

    def block(at, carry):
        first = pl.multiple_of(8 * at, 8)
        lines = pl.ds(first, 8)
        share = gain_ref[0, lines, 3 * POINTS :]
        for segment in range(1, 8):
            share = jnp.where(group == segment, gain_ref[segment, lines, 3 * POINTS :], share)
        keep = 1.0 - share
        for third in range(3):
            shifted = [gain_ref[segment, lines, third * POINTS : (third + 1) * POINTS] for segment in range(8)]
            for bit, mask in zip((1, 2, 4), bits):
                shifted = [jnp.where(mask, shifted[(i + bit) % 8], shifted[i]) for i in range(8)]
            for s in range(8):
                gained = shifted[-s % 8]
                if s:
                    gained = pltpu.roll(gained, POINTS - SEG * s, 1)
                write(8 * third + s, at, state_ref[8 * third + s, lines, :] * keep + gained)
        return carry

    lax.fori_loop(0, LINES // 8, block, 0, unroll=2)


def means_of(read):
    ones = jnp.full((8, 2 * POINTS), 1.0 / POINTS, BF16)
    rows = []
    for s in range(SPECIES):
        both = jnp.concatenate(halves(read(s)), axis=1)
        sums = lax.dot_general(ones, both, (((1,), (1,)), ((), ())), preferred_element_type=F32)
        rows.append(sums[:1])
    return jnp.concatenate(rows, axis=0)


def scales(diffusivity_row, eigen_row):
    row = jnp.concatenate([diffusivity_row, jnp.zeros((1, POINTS - SPECIES), F32)], axis=1)
    lane = iota(1, (SPECIES, POINTS))
    return jnp.where(lane == 0, 0.5, 1.0 / (1.0 + column(row)[:SPECIES] * eigen_row))


def first_mix_kernel(
    lines_hbm, start_hbm, diffusivity_hbm, eigen_hbm, first_hbm, second_hbm, rates_hbm, frozen_hbm,
    mixed_ref, high_ref, low_ref, scale_ref,
    lines_ref, start_ref, diffusivity_ref, eigen_ref, first_ref, second_ref, rates_ref, frozen_ref, index_ref, sems,
):
    here = [lines_ref.at[third].reshape(LINES, 8, POINTS) for third in range(3)]
    there = [lines_hbm.at[:, pl.ds(8 * third, 8), :] for third in range(3)]
    here += [rates_ref, frozen_ref, diffusivity_ref, eigen_ref, start_ref, first_ref, second_ref]
    there += [rates_hbm, frozen_hbm, diffusivity_hbm, eigen_hbm, start_hbm, first_hbm, second_hbm]
    copies = [pltpu.make_async_copy(a, b, sems.at[i]) for i, (a, b) in enumerate(zip(there, here))]
    for copy in copies:
        copy.start()
    for copy in copies:
        copy.wait()
    mix_tables(rates_ref[...], frozen_ref[...], high_ref, low_ref)
    scale_ref[...] = scales(diffusivity_ref[...], eigen_ref[...])

    def read(s):
        return lines_ref[s // 8, pl.ds(s % 8, LINES, stride=8), :]

    mixing(read, start_ref[0, 0], scale_ref, first_ref, second_ref, mixed_ref, index_ref)


def next_mix_kernel(
    state_ref, start_ref, scale_ref, first_ref, second_ref, from_ref, to_ref, codes_ref,
    mixed_ref, pick_ref, group_ref, hits_ref, index_ref,
):
    mixing(lambda s: state_ref[s], start_ref[1, 0], scale_ref, first_ref, second_ref, mixed_ref, index_ref)
    pick_tables(from_ref[1, 0], to_ref[1, 0], pick_ref, group_ref)
    hit_table([codes_ref[:1], codes_ref[1:2]], hits_ref)


def react(mixed_ref, les_ref, rim_refs, turns_ref, high_ref, low_ref, pick_ref, group_ref, state_ref, mid_ref, out_ref):
    mid = middle(les_ref[:, 0], *[ref[:, 0] for ref in rim_refs])
    mid_ref[...] = mid

    def finish(unit, values):
        pack_segments(unit, values, pick_ref, group_ref, out_ref)

    chemistry(turns_ref, turned(0.5 * mid), high_ref, low_ref, mixed_ref, state_ref, finish)


def first_react_kernel(
    mixed_ref, les_ref, line_even_ref, grid_odd_ref, line_odd_ref, grid_even_ref, high_ref, low_ref, owner_ref, line_ref,
    from_ref, to_ref, counts_ref, state_ref, send_ref, mid_ref, turns_ref, later_ref, out_ref, pick_ref, group_ref,
    placing_ref,
):
    turns_ref[...] = column(counts_ref[0])
    pick_tables(from_ref[0, 0], to_ref[0, 0], pick_ref, group_ref)
    place_tables(owner_ref[0, 0], placing_ref)
    place_tables(owner_ref[1, 0], later_ref)
    aims = [row for step in range(STEPS) for row in aim_rows(step, line_ref[step, 0], to_ref[step, 0])]
    placings = [ref[slot, :, :LINES] for ref in (placing_ref, later_ref) for slot in range(2)]
    rows = ROWS + AIMS
    send_ref[pl.ds(ROWS, OWNERS, stride=rows), :] = dot(
        jnp.concatenate(placings, axis=1), jnp.concatenate(aims, axis=0)
    )
    rim = (grid_even_ref, grid_odd_ref, line_even_ref, line_odd_ref)
    react(mixed_ref, les_ref, rim, turns_ref, high_ref, low_ref, pick_ref, group_ref, state_ref, mid_ref, out_ref)
    sending_rows(placing_ref, out_ref, send_ref, rows)


def next_react_kernel(
    mixed_ref, les_ref, grid_even_ref, line_even_ref, grid_odd_ref, line_odd_ref, high_ref, low_ref, pick_ref, group_ref,
    turns_ref, placing_ref, state_ref, send_ref, mid_ref, out_ref,
):
    rim = (grid_even_ref, grid_odd_ref, line_even_ref, line_odd_ref)
    react(mixed_ref, les_ref, rim, turns_ref, high_ref, low_ref, pick_ref, group_ref, state_ref, mid_ref, out_ref)
    sending_rows(placing_ref, out_ref, send_ref, ROWS)


def next_splice_kernel(received_ref, state_ref, mid_ref, les_ref, lines_ref, codes_ref, parts_ref, gain_ref, hits_ref):
    def write(species, at, value):
        lines_ref[species, pl.ds(pl.multiple_of(8 * at, 8), 8), :] = value

    rows = ROWS + AIMS
    codes = aim_codes(received_ref[pl.ds(ROWS, OWNERS, stride=rows), :])
    codes_ref[...] = jnp.concatenate(codes[1] + [jnp.zeros((6, OWNERS), F32)], axis=0)
    hit_table(codes[0], hits_ref)
    splicing(received_ref, rows, state_ref, write, parts_ref, hits_ref, gain_ref)
    les_ref[:, 0] = 0.5 * mid_ref[...] + 0.5 * means_of(lambda s: lines_ref[s])


def last_splice_kernel(
    received_ref, state_ref, mid_ref, hits_ref, les_ref, lines_hbm, parts_ref, gain_ref, lines_ref, sems
):
    rows = 8 * SPECIES

    def out(at):
        part = pl.ds(pl.multiple_of(at * rows, rows), rows)
        return pltpu.make_async_copy(lines_ref.at[part], lines_hbm.at[part], sems.at[at])

    def write(species, at, value):
        lines_ref[pl.ds(at * rows + species, 8, stride=SPECIES), :] = value
        if species == SPECIES - 1:
            out(at).start()

    splicing(received_ref, ROWS, state_ref, write, parts_ref, hits_ref, gain_ref)
    means = means_of(lambda s: lines_ref[pl.ds(s, LINES, stride=SPECIES), :])
    les_ref[:, 0] = 0.5 * mid_ref[...] + 0.5 * means
    for at in range(LINES // 8):
        out(at).wait()


VMEM = pl.BlockSpec(memory_space=pltpu.VMEM)
HBM = pl.BlockSpec(memory_space=pltpu.HBM)
STATE = jax.ShapeDtypeStruct((SPECIES, LINES, POINTS), F32)
FLAT = jax.ShapeDtypeStruct((LINES * SPECIES, POINTS), F32)
SPLICE_SCRATCH = [pltpu.VMEM((4 * OWNERS, 4 * POINTS), BF16), pltpu.VMEM((8, LINES, 4 * POINTS), F32)]


def call(kernel, inputs, outputs, scratch, micros, in_space=VMEM, out_specs=None):
    size = sum(x.size * x.dtype.itemsize for x in [*inputs, *outputs])
    if in_space is HBM:
        inputs = [pltpu.with_memory_space_constraint(x, pltpu.HBM) for x in inputs]
    return pl.pallas_call(
        kernel,
        out_shape=outputs,
        in_specs=[in_space] * len(inputs),
        out_specs=out_specs or [VMEM] * len(outputs),
        scratch_shapes=scratch,
        cost_estimate=pl.CostEstimate(flops=micros * 10**9, bytes_accessed=size, transcendentals=0),
        compiler_params=pltpu.CompilerParams(vmem_limit_bytes=32 << 20),
    )(*inputs)


def beside(field):
    around = []
    for axis in ("grid", "line"):
        peers = lax.axis_size(axis)
        for start in (0, 1):
            pairs = [(i, (i + 1) % peers) for i in range(start, peers, 2)]
            around.append(lax.ppermute(field, axis, pairs + [(b, a) for a, b in pairs]))
    return around


def body(
    les,
    lines,
    triplet_start,
    splice_owner,
    splice_line,
    splice_from,
    splice_to,
    chem_counts,
    diffusivity,
    rates,
    frozen_inverse,
):
    def shaped(shape, dtype=F32):
        return jax.ShapeDtypeStruct(shape, dtype)

    first_table, second_table, eigen = (jnp.asarray(x) for x in cosine_tables())
    side = SPECIES * 8
    plane = shaped((SPECIES, LINES))
    owner = splice_owner.reshape(STEPS, 1, 1, LINES)
    square = shaped((LINES, POINTS))
    index = shaped((LINES, POINTS), jnp.int32)
    placing = shaped((2, OWNERS, 2 * LINES), BF16)
    hits = shaped((8 * LINES, 4 * OWNERS), BF16)
    scratch_of = lambda x: pltpu.VMEM(x.shape, x.dtype)
    outgoing = pltpu.VMEM((2 * LINES, 3 * POINTS), BF16)

    def exchange(sending):
        sending = sending.reshape(OWNERS, 1, -1)
        received = lax.all_to_all(sending, ("grid", "line"), split_axis=0, concat_axis=0, tiled=True)
        return received.reshape(-1, POINTS)

    grid_even, grid_odd, line_even, line_odd = beside(les)
    inputs = [lines.reshape(LINES, SPECIES, POINTS), triplet_start, diffusivity.reshape(1, SPECIES), eigen]
    inputs += [first_table, second_table, rates, frozen_inverse]
    scratch = [pltpu.VMEM((3, LINES * 8, POINTS), F32)] + [scratch_of(x) for x in inputs[1:]]
    scratch += [scratch_of(index), pltpu.SemaphoreType.DMA((len(inputs) + 2,))]
    table = shaped((side, side), BF16)
    mixed, high, low, scale = call(first_mix_kernel, inputs, [STATE, table, table, plane], scratch, 4, in_space=HBM)

    inputs = [mixed, les, line_even, grid_odd, line_odd, grid_even, high, low, owner, splice_line, splice_from, splice_to, chem_counts]
    outputs = [STATE, shaped((OWNERS * (ROWS + AIMS), POINTS)), plane, square, placing]
    scratch = [outgoing, scratch_of(index), scratch_of(index), scratch_of(placing)]
    state, sending, mid, turns, later = call(first_react_kernel, inputs, outputs, scratch, 6)

    inputs = [exchange(sending), state, mid]
    outputs = [shaped(les.shape), STATE, shaped((8, OWNERS))]
    field, state, codes = call(next_splice_kernel, inputs, outputs, SPLICE_SCRATCH + [scratch_of(hits)], 3)

    grid_even, grid_odd, line_even, line_odd = beside(field)
    inputs = [state, triplet_start, scale, first_table, second_table, splice_from, splice_to, codes]
    mixed, pick, group, landing = call(
        next_mix_kernel, inputs, [STATE, index, index, hits], [scratch_of(index)], 3
    )

    inputs = [mixed, field, grid_even, line_even, grid_odd, line_odd, high, low, pick, group, turns, later]
    outputs = [STATE, shaped((OWNERS * ROWS, POINTS)), plane]
    state, sending, mid = call(next_react_kernel, inputs, outputs, [outgoing], 6)

    inputs = [exchange(sending), state, mid, landing]
    outputs = [shaped(les.shape), FLAT]
    scratch = SPLICE_SCRATCH + [scratch_of(FLAT), pltpu.SemaphoreType.DMA((LINES // 8,))]
    field, state = call(last_splice_kernel, inputs, outputs, scratch, 3, out_specs=[VMEM, HBM])
    return (field, state.reshape(lines.shape))


def solution(mesh):
    in_specs = (
        P(None, "grid", "line"),
        P("grid", "line", None, None, None),
        P(None, "grid", "line", None),
        P(None, "grid", "line", None, None),
        P(None, "grid", "line", None),
        P(None, "grid", "line", None),
        P(None, "grid", "line", None),
        P("grid", "line", None),
        P(),
        P(),
        P(),
    )
    out_specs = (P(None, "grid", "line"), P("grid", "line", None, None, None))
    return jax.shard_map(body, mesh=mesh, in_specs=in_specs, out_specs=out_specs, check_vma=False)
```

```python
import jax
import jax.numpy as jnp
import numpy as np
from jax import lax
from jax.experimental import pallas as pl
from jax.experimental.pallas import tpu as pltpu
from jax.sharding import PartitionSpec as P

SEG = 16
TRIP = 48
KMAX = 6
STEPS = 2
LES_RATE = 0.2
SPECIES = 24
POINTS = 128
LINES = 128
OWNERS = 128
ROWS = 6
AIMS = 1
F32 = jnp.float32
BF16 = jnp.bfloat16


def cosine_tables():
    k = np.arange(POINTS)[:, None]
    p = np.arange(POINTS)[None, :]
    basis = np.sqrt(2.0 / POINTS) * np.cos(np.pi * k * (2 * p + 1) / (2 * POINTS))
    basis[0] = 1.0 / np.sqrt(POINTS)
    tables = []
    for table in (basis.T, basis):
        high = table.astype(BF16)
        low = (table - high.astype(np.float64)).astype(BF16)
        half = np.concatenate([high, low], axis=1)
        tables.append(np.concatenate([half, half], axis=0))
    eigen = 4.0 * np.sin(np.pi * np.arange(POINTS) / (2 * POINTS)) ** 2
    return tables[0], tables[1], eigen.astype(np.float32)[None, :]


def halves(value):
    high = value.astype(BF16)
    return high, (value - high.astype(F32)).astype(BF16)


def dot(a, b):
    return jnp.dot(a, b, preferred_element_type=F32)


def iota(axis, shape=(LINES, POINTS)):
    return lax.broadcasted_iota(jnp.int32, shape, axis)


def column(row):
    return jnp.transpose(jnp.broadcast_to(row.astype(F32), (LINES, POINTS)))


def lane_pick(value, index):
    return jnp.take_along_axis(value, index, axis=1, mode="promise_in_bounds")


def mix_tables(rates, frozen, high_ref, low_ref):
    exact = dict(precision=lax.Precision.HIGHEST, preferred_element_type=F32)
    matrix = jnp.dot(frozen, rates, **exact)
    side = SPECIES * 8
    spread = (iota(0, (side, SPECIES)) // 8 == iota(1, (side, SPECIES))).astype(F32)
    gather = (iota(0, (SPECIES, side)) == iota(1, (SPECIES, side)) // 8).astype(F32)
    wide = jnp.dot(jnp.dot(spread, matrix, **exact), gather, **exact)
    same = iota(0, (side, side)) % 8 == iota(1, (side, side)) % 8
    high, low = halves(jnp.where(same, wide, 0.0))
    high_ref[...] = high
    low_ref[...] = low


def middle(les, grid_even, grid_odd, line_even, line_odd):
    row, place = lax.axis_index("grid"), lax.axis_index("line")
    inner = jnp.logical_and(row > 0, row < lax.axis_size("grid") - 1)
    even = place % 2 == 0
    west = jnp.where(even, line_odd, line_even)
    east = jnp.where(even, line_even, line_odd)
    west = jnp.where(place > 0, west, 0.0)
    east = jnp.where(place < lax.axis_size("line") - 1, east, 0.0)
    lane = iota(1, (SPECIES, LINES))
    left = jnp.where(lane == 0, pltpu.roll(west, 1, 1), pltpu.roll(les, 1, 1))
    right = jnp.where(lane == LINES - 1, pltpu.roll(east, LINES - 1, 1), pltpu.roll(les, LINES - 1, 1))
    return les + LES_RATE * (grid_even + jnp.where(inner, grid_odd, 0.0) + left + right - 4.0 * les)


def turned(value):
    pad = jnp.zeros((POINTS - SPECIES, LINES), F32)
    return jnp.transpose(jnp.concatenate([value, pad], axis=0))


def triplet_index(start):
    place = iota(1)
    start = start.astype(jnp.int32)
    rel = place - start
    third = TRIP // 3
    source = jnp.where(
        rel < third,
        3 * rel,
        jnp.where(rel < 2 * third, 3 * (2 * third - 1 - rel) + 1, 3 * (rel - 2 * third) + 2),
    )
    return jnp.where((rel >= 0) & (rel < TRIP), source + start, place)


def mixing(read, start_row, scale_ref, first_ref, second_ref, state_ref, index_ref):
    index_ref[...] = triplet_index(column(start_row))
    group = 8

    for at in range(SPECIES // group):
        species = [at * group + i for i in range(group)]
        value = jnp.concatenate([lane_pick(read(s), index_ref[...]) for s in species], axis=0)
        wide = dot(jnp.concatenate(halves(value), axis=1), first_ref[...])
        value = wide[:, :POINTS] + wide[:, POINTS:]
        value = value.reshape(group, LINES, POINTS)
        value = jnp.concatenate([value[i] * scale_ref[s : s + 1, :] for i, s in enumerate(species)], axis=0)
        wide = dot(jnp.concatenate(halves(value), axis=1), second_ref[...])
        value = (wide[:, :POINTS] + wide[:, POINTS:]).reshape(group, LINES, POINTS)
        for i, s in enumerate(species):
            state_ref[s] = value[i]


def chemistry(turns_ref, shift, high_ref, low_ref, mixed_ref, state_ref, finish):
    side = SPECIES * 8

    def shifted(part):
        rows = [jnp.broadcast_to(shift[part, s : s + 1], (8, POINTS))[None] for s in range(SPECIES)]
        return mixed_ref[:, part, :] + jnp.concatenate(rows, axis=0)

    for turn in range(KMAX):
        for unit in range(LINES // 16):
            parts = [slice(16 * unit, 16 * unit + 8), slice(16 * unit + 8, 16 * unit + 16)]
            old = [(state_ref[:, part, :] if turn else shifted(part)).reshape(side, POINTS) for part in parts]
            high, low = halves(jnp.tanh(jnp.concatenate(old, axis=1)))
            change = dot(high_ref[...], high) + (dot(low_ref[...], high) + dot(high_ref[...], low))
            done = []
            for at, part in enumerate(parts):
                active = (turns_ref[part, :] > float(turn))[None]
                before = old[at].reshape(SPECIES, 8, POINTS)
                after = before + change[:, at * POINTS : (at + 1) * POINTS].reshape(SPECIES, 8, POINTS)
                done.append(jnp.where(active, after, before))
                state_ref[:, part, :] = done[at]
            if turn == KMAX - 1:
                finish(unit, done)


def pick_tables(from_row, to_row, pick_ref, group_ref):
    lane = iota(1)
    pick_ref[...] = column(from_row).astype(jnp.int32) * SEG + lane % SEG
    group_ref[...] = (lane // SEG - column(to_row).astype(jnp.int32)) & 7


def place_tables(owner_row, placing_ref):
    lane = iota(1)
    owner = column(owner_row).astype(jnp.int32)
    earlier = (owner == owner_row) & (iota(0) < lane)
    rank = jnp.sum(earlier.astype(F32), axis=0, keepdims=True)
    for slot in range(2):
        placing = ((iota(0) == owner_row) & (rank == slot)).astype(F32).astype(BF16)
        placing_ref[slot, :, :LINES] = placing
        placing_ref[slot, :, LINES:] = placing


def aim_rows(step, line_row, to_row):
    lane = iota(1)
    line, segment = column(line_row) + 1.0, column(to_row)
    rows = []
    for slot in range(2):
        at = 4 * step + 2 * slot
        rows.append(jnp.where(lane // SEG == at, line, jnp.where(lane // SEG == at + 1, segment, 0.0)).astype(BF16))
    return rows


def aim_codes(aims):
    turned_aims = jnp.transpose(aims)

    def code(at):
        line, segment = turned_aims[SEG * at : SEG * at + 1], turned_aims[SEG * at + SEG : SEG * at + SEG + 1]
        return segment * LINES + line - 1.0

    return [[code(4 * step + 2 * slot) for slot in range(2)] for step in range(STEPS)]


def hit_table(codes, hits_ref):
    place = iota(0).astype(F32)
    for slot in range(2):
        for segment in range(8):
            hit = jnp.where(place + float(segment * LINES) == codes[slot], 0.5, 0.0).astype(BF16)
            for at in (slot, 2 + slot):
                hits_ref[segment * LINES : (segment + 1) * LINES, at * OWNERS : (at + 1) * OWNERS] = hit


def pack_segments(unit, values, pick_ref, group_ref, out_ref):
    parts = [slice(16 * unit, 16 * unit + 8), slice(16 * unit + 8, 16 * unit + 16)]
    for third in range(3):
        halves_of = []
        for part, value in zip(parts, values):
            pick, group = pick_ref[part, :], group_ref[part, :]
            gathered = lane_pick(value[8 * third], pick)
            for s in range(1, 8):
                gathered = jnp.where(group == s, lane_pick(value[8 * third + s], pick), gathered)
            halves_of.append(gathered)
        high, low = halves(jnp.concatenate(halves_of, axis=0))
        columns = slice(third * POINTS, (third + 1) * POINTS)
        out_ref[16 * unit : 16 * unit + 16, columns] = high
        out_ref[LINES + 16 * unit : LINES + 16 * unit + 16, columns] = low


def sending_rows(placing_ref, out_ref, send_ref, rows):
    for slot in range(2):
        sending = dot(placing_ref[slot], out_ref[...])
        for third in range(3):
            send_ref[pl.ds(3 * slot + third, OWNERS, stride=rows), :] = sending[
                :, third * POINTS : (third + 1) * POINTS
            ]


def splicing(received_ref, rows, state_ref, write, parts_ref, hits_ref, gain_ref):
    for slot in range(2):
        highs = slice(slot * OWNERS, (slot + 1) * OWNERS)
        lows = slice((2 + slot) * OWNERS, (3 + slot) * OWNERS)
        for third in range(3):
            high, low = halves(received_ref[pl.ds(3 * slot + third, OWNERS, stride=rows), :])
            parts_ref[highs, third * POINTS : (third + 1) * POINTS] = high
            parts_ref[lows, third * POINTS : (third + 1) * POINTS] = low
        parts_ref[highs, 3 * POINTS :] = jnp.ones((OWNERS, POINTS), BF16)
        parts_ref[lows, 3 * POINTS :] = jnp.zeros((OWNERS, POINTS), BF16)
    gain_ref[...] = dot(hits_ref[...], parts_ref[...]).reshape(8, LINES, 4 * POINTS)
    group = iota(1, (8, POINTS)) // SEG
    bits = [(group & bit) != 0 for bit in (1, 2, 4)]

    def block(at, carry):
        first = pl.multiple_of(8 * at, 8)
        lines = pl.ds(first, 8)
        share = gain_ref[0, lines, 3 * POINTS :]
        for segment in range(1, 8):
            share = jnp.where(group == segment, gain_ref[segment, lines, 3 * POINTS :], share)
        keep = 1.0 - share
        for third in range(3):
            shifted = [gain_ref[segment, lines, third * POINTS : (third + 1) * POINTS] for segment in range(8)]
            for bit, mask in zip((1, 2, 4), bits):
                shifted = [jnp.where(mask, shifted[(i + bit) % 8], shifted[i]) for i in range(8)]
            for s in range(8):
                gained = shifted[-s % 8]
                if s:
                    gained = pltpu.roll(gained, POINTS - SEG * s, 1)
                write(8 * third + s, at, state_ref[8 * third + s, lines, :] * keep + gained)
        return carry

    lax.fori_loop(0, LINES // 8, block, 0, unroll=8)


def means_of(read):
    ones = jnp.full((8, 2 * POINTS), 1.0 / POINTS, BF16)
    rows = []
    for s in range(SPECIES):
        both = jnp.concatenate(halves(read(s)), axis=1)
        sums = lax.dot_general(ones, both, (((1,), (1,)), ((), ())), preferred_element_type=F32)
        rows.append(sums[:1])
    return jnp.concatenate(rows, axis=0)


def scales(diffusivity_row, eigen_row):
    row = jnp.concatenate([diffusivity_row, jnp.zeros((1, POINTS - SPECIES), F32)], axis=1)
    lane = iota(1, (SPECIES, POINTS))
    return jnp.where(lane == 0, 0.5, 1.0 / (1.0 + column(row)[:SPECIES] * eigen_row))


def first_mix_kernel(
    lines_hbm, start_hbm, diffusivity_hbm, eigen_hbm, first_hbm, second_hbm, rates_hbm, frozen_hbm,
    mixed_ref, high_ref, low_ref, scale_ref,
    lines_ref, start_ref, diffusivity_ref, eigen_ref, first_ref, second_ref, rates_ref, frozen_ref, index_ref, sems,
):
    here = [lines_ref.at[third].reshape(LINES, 8, POINTS) for third in range(3)]
    there = [lines_hbm.at[:, pl.ds(8 * third, 8), :] for third in range(3)]
    here += [rates_ref, frozen_ref, diffusivity_ref, eigen_ref, start_ref, first_ref, second_ref]
    there += [rates_hbm, frozen_hbm, diffusivity_hbm, eigen_hbm, start_hbm, first_hbm, second_hbm]
    copies = [pltpu.make_async_copy(a, b, sems.at[i]) for i, (a, b) in enumerate(zip(there, here))]
    for copy in copies:
        copy.start()
    for copy in copies:
        copy.wait()
    mix_tables(rates_ref[...], frozen_ref[...], high_ref, low_ref)
    scale_ref[...] = scales(diffusivity_ref[...], eigen_ref[...])

    def read(s):
        return lines_ref[s // 8, pl.ds(s % 8, LINES, stride=8), :]

    mixing(read, start_ref[0, 0], scale_ref, first_ref, second_ref, mixed_ref, index_ref)


def next_mix_kernel(
    state_ref, start_ref, scale_ref, first_ref, second_ref, from_ref, to_ref, codes_ref,
    mixed_ref, pick_ref, group_ref, hits_ref, index_ref,
):
    mixing(lambda s: state_ref[s], start_ref[1, 0], scale_ref, first_ref, second_ref, mixed_ref, index_ref)
    pick_tables(from_ref[1, 0], to_ref[1, 0], pick_ref, group_ref)
    hit_table([codes_ref[:1], codes_ref[1:2]], hits_ref)


def react(mixed_ref, les_ref, rim_refs, turns_ref, high_ref, low_ref, pick_ref, group_ref, state_ref, mid_ref, out_ref):
    mid = middle(les_ref[:, 0], *[ref[:, 0] for ref in rim_refs])
    mid_ref[...] = mid

    def finish(unit, values):
        pack_segments(unit, values, pick_ref, group_ref, out_ref)

    chemistry(turns_ref, turned(0.5 * mid), high_ref, low_ref, mixed_ref, state_ref, finish)


def first_react_kernel(
    mixed_ref, les_ref, line_even_ref, grid_odd_ref, line_odd_ref, grid_even_ref, high_ref, low_ref, owner_ref, line_ref,
    from_ref, to_ref, counts_ref, state_ref, send_ref, mid_ref, turns_ref, later_ref, out_ref, pick_ref, group_ref,
    placing_ref,
):
    turns_ref[...] = column(counts_ref[0])
    pick_tables(from_ref[0, 0], to_ref[0, 0], pick_ref, group_ref)
    place_tables(owner_ref[0, 0], placing_ref)
    place_tables(owner_ref[1, 0], later_ref)
    aims = [row for step in range(STEPS) for row in aim_rows(step, line_ref[step, 0], to_ref[step, 0])]
    placings = [ref[slot, :, :LINES] for ref in (placing_ref, later_ref) for slot in range(2)]
    rows = ROWS + AIMS
    send_ref[pl.ds(ROWS, OWNERS, stride=rows), :] = dot(
        jnp.concatenate(placings, axis=1), jnp.concatenate(aims, axis=0)
    )
    rim = (grid_even_ref, grid_odd_ref, line_even_ref, line_odd_ref)
    react(mixed_ref, les_ref, rim, turns_ref, high_ref, low_ref, pick_ref, group_ref, state_ref, mid_ref, out_ref)
    sending_rows(placing_ref, out_ref, send_ref, rows)


def next_react_kernel(
    mixed_ref, les_ref, grid_even_ref, line_even_ref, grid_odd_ref, line_odd_ref, high_ref, low_ref, pick_ref, group_ref,
    turns_ref, placing_ref, state_ref, send_ref, mid_ref, out_ref,
):
    rim = (grid_even_ref, grid_odd_ref, line_even_ref, line_odd_ref)
    react(mixed_ref, les_ref, rim, turns_ref, high_ref, low_ref, pick_ref, group_ref, state_ref, mid_ref, out_ref)
    sending_rows(placing_ref, out_ref, send_ref, ROWS)


def next_splice_kernel(received_ref, state_ref, mid_ref, les_ref, lines_ref, codes_ref, parts_ref, gain_ref, hits_ref):
    def write(species, at, value):
        lines_ref[species, pl.ds(pl.multiple_of(8 * at, 8), 8), :] = value

    rows = ROWS + AIMS
    codes = aim_codes(received_ref[pl.ds(ROWS, OWNERS, stride=rows), :])
    codes_ref[...] = jnp.concatenate(codes[1] + [jnp.zeros((6, OWNERS), F32)], axis=0)
    hit_table(codes[0], hits_ref)
    splicing(received_ref, rows, state_ref, write, parts_ref, hits_ref, gain_ref)
    les_ref[:, 0] = 0.5 * mid_ref[...] + 0.5 * means_of(lambda s: lines_ref[s])


def last_splice_kernel(
    received_ref, state_ref, mid_ref, hits_ref, les_ref, lines_hbm, parts_ref, gain_ref, lines_ref, sems
):
    rows = 8 * SPECIES

    def out(at):
        part = pl.ds(pl.multiple_of(at * rows, rows), rows)
        return pltpu.make_async_copy(lines_ref.at[part], lines_hbm.at[part], sems.at[at])

    def write(species, at, value):
        lines_ref[pl.ds(at * rows + species, 8, stride=SPECIES), :] = value
        if species == SPECIES - 1:
            out(at).start()

    splicing(received_ref, ROWS, state_ref, write, parts_ref, hits_ref, gain_ref)
    means = means_of(lambda s: lines_ref[pl.ds(s, LINES, stride=SPECIES), :])
    les_ref[:, 0] = 0.5 * mid_ref[...] + 0.5 * means
    for at in range(LINES // 8):
        out(at).wait()


VMEM = pl.BlockSpec(memory_space=pltpu.VMEM)
HBM = pl.BlockSpec(memory_space=pltpu.HBM)
STATE = jax.ShapeDtypeStruct((SPECIES, LINES, POINTS), F32)
FLAT = jax.ShapeDtypeStruct((LINES * SPECIES, POINTS), F32)
SPLICE_SCRATCH = [pltpu.VMEM((4 * OWNERS, 4 * POINTS), BF16), pltpu.VMEM((8, LINES, 4 * POINTS), F32)]


def call(kernel, inputs, outputs, scratch, micros, in_space=VMEM, out_specs=None):
    size = sum(x.size * x.dtype.itemsize for x in [*inputs, *outputs])
    if in_space is HBM:
        inputs = [pltpu.with_memory_space_constraint(x, pltpu.HBM) for x in inputs]
    return pl.pallas_call(
        kernel,
        out_shape=outputs,
        in_specs=[in_space] * len(inputs),
        out_specs=out_specs or [VMEM] * len(outputs),
        scratch_shapes=scratch,
        cost_estimate=pl.CostEstimate(flops=micros * 10**9, bytes_accessed=size, transcendentals=0),
        compiler_params=pltpu.CompilerParams(vmem_limit_bytes=32 << 20),
    )(*inputs)


def beside(field):
    around = []
    for axis in ("grid", "line"):
        peers = lax.axis_size(axis)
        for start in (0, 1):
            pairs = [(i, (i + 1) % peers) for i in range(start, peers, 2)]
            around.append(lax.ppermute(field, axis, pairs + [(b, a) for a, b in pairs]))
    return around


def body(
    les,
    lines,
    triplet_start,
    splice_owner,
    splice_line,
    splice_from,
    splice_to,
    chem_counts,
    diffusivity,
    rates,
    frozen_inverse,
):
    def shaped(shape, dtype=F32):
        return jax.ShapeDtypeStruct(shape, dtype)

    first_table, second_table, eigen = (jnp.asarray(x) for x in cosine_tables())
    side = SPECIES * 8
    plane = shaped((SPECIES, LINES))
    owner = splice_owner.reshape(STEPS, 1, 1, LINES)
    square = shaped((LINES, POINTS))
    index = shaped((LINES, POINTS), jnp.int32)
    placing = shaped((2, OWNERS, 2 * LINES), BF16)
    hits = shaped((8 * LINES, 4 * OWNERS), BF16)
    scratch_of = lambda x: pltpu.VMEM(x.shape, x.dtype)
    outgoing = pltpu.VMEM((2 * LINES, 3 * POINTS), BF16)

    def exchange(sending):
        sending = sending.reshape(OWNERS, 1, -1)
        received = lax.all_to_all(sending, ("grid", "line"), split_axis=0, concat_axis=0, tiled=True)
        return received.reshape(-1, POINTS)

    grid_even, grid_odd, line_even, line_odd = beside(les)
    inputs = [lines.reshape(LINES, SPECIES, POINTS), triplet_start, diffusivity.reshape(1, SPECIES), eigen]
    inputs += [first_table, second_table, rates, frozen_inverse]
    scratch = [pltpu.VMEM((3, LINES * 8, POINTS), F32)] + [scratch_of(x) for x in inputs[1:]]
    scratch += [scratch_of(index), pltpu.SemaphoreType.DMA((len(inputs) + 2,))]
    table = shaped((side, side), BF16)
    mixed, high, low, scale = call(first_mix_kernel, inputs, [STATE, table, table, plane], scratch, 4, in_space=HBM)

    inputs = [mixed, les, line_even, grid_odd, line_odd, grid_even, high, low, owner, splice_line, splice_from, splice_to, chem_counts]
    outputs = [STATE, shaped((OWNERS * (ROWS + AIMS), POINTS)), plane, square, placing]
    scratch = [outgoing, scratch_of(index), scratch_of(index), scratch_of(placing)]
    state, sending, mid, turns, later = call(first_react_kernel, inputs, outputs, scratch, 6)

    inputs = [exchange(sending), state, mid]
    outputs = [shaped(les.shape), STATE, shaped((8, OWNERS))]
    field, state, codes = call(next_splice_kernel, inputs, outputs, SPLICE_SCRATCH + [scratch_of(hits)], 3)

    grid_even, grid_odd, line_even, line_odd = beside(field)
    inputs = [state, triplet_start, scale, first_table, second_table, splice_from, splice_to, codes]
    mixed, pick, group, landing = call(
        next_mix_kernel, inputs, [STATE, index, index, hits], [scratch_of(index)], 3
    )

    inputs = [mixed, field, grid_even, line_even, grid_odd, line_odd, high, low, pick, group, turns, later]
    outputs = [STATE, shaped((OWNERS * ROWS, POINTS)), plane]
    state, sending, mid = call(next_react_kernel, inputs, outputs, [outgoing], 6)

    inputs = [exchange(sending), state, mid, landing]
    outputs = [shaped(les.shape), FLAT]
    scratch = SPLICE_SCRATCH + [scratch_of(FLAT), pltpu.SemaphoreType.DMA((LINES // 8,))]
    field, state = call(last_splice_kernel, inputs, outputs, scratch, 3, out_specs=[VMEM, HBM])
    return (field, state.reshape(lines.shape))


def solution(mesh):
    in_specs = (
        P(None, "grid", "line"),
        P("grid", "line", None, None, None),
        P(None, "grid", "line", None),
        P(None, "grid", "line", None, None),
        P(None, "grid", "line", None),
        P(None, "grid", "line", None),
        P(None, "grid", "line", None),
        P("grid", "line", None),
        P(),
        P(),
        P(),
    )
    out_specs = (P(None, "grid", "line"), P("grid", "line", None, None, None))
    return jax.shard_map(body, mesh=mesh, in_specs=in_specs, out_specs=out_specs, check_vma=False)
```

```python
import jax
import jax.numpy as jnp
import numpy as np
from jax import lax
from jax.experimental import pallas as pl
from jax.experimental.pallas import tpu as pltpu
from jax.sharding import PartitionSpec as P

SEG = 16
TRIP = 48
KMAX = 6
STEPS = 2
LES_RATE = 0.2
SPECIES = 24
POINTS = 128
LINES = 128
OWNERS = 128
ROWS = 6
AIMS = 1
F32 = jnp.float32
BF16 = jnp.bfloat16


def cosine_tables():
    k = np.arange(POINTS)[:, None]
    p = np.arange(POINTS)[None, :]
    basis = np.sqrt(2.0 / POINTS) * np.cos(np.pi * k * (2 * p + 1) / (2 * POINTS))
    basis[0] = 1.0 / np.sqrt(POINTS)
    tables = []
    for table in (basis.T, basis):
        high = table.astype(BF16)
        low = (table - high.astype(np.float64)).astype(BF16)
        half = np.concatenate([high, low], axis=1)
        tables.append(np.concatenate([half, half], axis=0))
    eigen = 4.0 * np.sin(np.pi * np.arange(POINTS) / (2 * POINTS)) ** 2
    return tables[0], tables[1], eigen.astype(np.float32)[None, :]


def halves(value):
    high = value.astype(BF16)
    return high, (value - high.astype(F32)).astype(BF16)


def dot(a, b):
    return jnp.dot(a, b, preferred_element_type=F32)


def iota(axis, shape=(LINES, POINTS)):
    return lax.broadcasted_iota(jnp.int32, shape, axis)


def column(row):
    return jnp.transpose(jnp.broadcast_to(row.astype(F32), (LINES, POINTS)))


def lane_pick(value, index):
    return jnp.take_along_axis(value, index, axis=1, mode="promise_in_bounds")


def mix_tables(rates, frozen, high_ref, low_ref):
    exact = dict(precision=lax.Precision.HIGHEST, preferred_element_type=F32)
    matrix = jnp.dot(frozen, rates, **exact)
    side = SPECIES * 8
    spread = (iota(0, (side, SPECIES)) // 8 == iota(1, (side, SPECIES))).astype(F32)
    gather = (iota(0, (SPECIES, side)) == iota(1, (SPECIES, side)) // 8).astype(F32)
    wide = jnp.dot(jnp.dot(spread, matrix, **exact), gather, **exact)
    same = iota(0, (side, side)) % 8 == iota(1, (side, side)) % 8
    high, low = halves(jnp.where(same, wide, 0.0))
    high_ref[...] = high
    low_ref[...] = low


def middle(les, grid_even, grid_odd, line_even, line_odd):
    row, place = lax.axis_index("grid"), lax.axis_index("line")
    inner = jnp.logical_and(row > 0, row < lax.axis_size("grid") - 1)
    even = place % 2 == 0
    west = jnp.where(even, line_odd, line_even)
    east = jnp.where(even, line_even, line_odd)
    west = jnp.where(place > 0, west, 0.0)
    east = jnp.where(place < lax.axis_size("line") - 1, east, 0.0)
    lane = iota(1, (SPECIES, LINES))
    left = jnp.where(lane == 0, pltpu.roll(west, 1, 1), pltpu.roll(les, 1, 1))
    right = jnp.where(lane == LINES - 1, pltpu.roll(east, LINES - 1, 1), pltpu.roll(les, LINES - 1, 1))
    return les + LES_RATE * (grid_even + jnp.where(inner, grid_odd, 0.0) + left + right - 4.0 * les)


def turned(value):
    pad = jnp.zeros((POINTS - SPECIES, LINES), F32)
    return jnp.transpose(jnp.concatenate([value, pad], axis=0))


def triplet_index(start):
    place = iota(1)
    start = start.astype(jnp.int32)
    rel = place - start
    third = TRIP // 3
    source = jnp.where(
        rel < third,
        3 * rel,
        jnp.where(rel < 2 * third, 3 * (2 * third - 1 - rel) + 1, 3 * (rel - 2 * third) + 2),
    )
    return jnp.where((rel >= 0) & (rel < TRIP), source + start, place)


def mixing(read, start_row, scale_ref, first_ref, second_ref, state_ref, index_ref):
    index_ref[...] = triplet_index(column(start_row))
    group = 8

    for at in range(SPECIES // group):
        species = [at * group + i for i in range(group)]
        value = jnp.concatenate([lane_pick(read(s), index_ref[...]) for s in species], axis=0)
        wide = dot(jnp.concatenate(halves(value), axis=1), first_ref[...])
        value = wide[:, :POINTS] + wide[:, POINTS:]
        value = value.reshape(group, LINES, POINTS)
        value = jnp.concatenate([value[i] * scale_ref[s : s + 1, :] for i, s in enumerate(species)], axis=0)
        wide = dot(jnp.concatenate(halves(value), axis=1), second_ref[...])
        value = (wide[:, :POINTS] + wide[:, POINTS:]).reshape(group, LINES, POINTS)
        for i, s in enumerate(species):
            state_ref[s] = value[i]


def chemistry(turns_ref, shift, high_ref, low_ref, mixed_ref, state_ref, finish):
    side = SPECIES * 8

    def shifted(part):
        rows = [jnp.broadcast_to(shift[part, s : s + 1], (8, POINTS))[None] for s in range(SPECIES)]
        return mixed_ref[:, part, :] + jnp.concatenate(rows, axis=0)

    for turn in range(KMAX):
        for unit in range(LINES // 16):
            parts = [slice(16 * unit, 16 * unit + 8), slice(16 * unit + 8, 16 * unit + 16)]
            old = [(state_ref[:, part, :] if turn else shifted(part)).reshape(side, POINTS) for part in parts]
            high, low = halves(jnp.tanh(jnp.concatenate(old, axis=1)))
            change = dot(high_ref[...], high) + (dot(low_ref[...], high) + dot(high_ref[...], low))
            done = []
            for at, part in enumerate(parts):
                active = (turns_ref[part, :] > float(turn))[None]
                before = old[at].reshape(SPECIES, 8, POINTS)
                after = before + change[:, at * POINTS : (at + 1) * POINTS].reshape(SPECIES, 8, POINTS)
                done.append(jnp.where(active, after, before))
                state_ref[:, part, :] = done[at]
            if turn == KMAX - 1:
                finish(unit, done)


def pick_tables(from_row, to_row, pick_ref, group_ref):
    lane = iota(1)
    pick_ref[...] = column(from_row).astype(jnp.int32) * SEG + lane % SEG
    group_ref[...] = (lane // SEG - column(to_row).astype(jnp.int32)) & 7


def place_tables(owner_row, placing_ref):
    lane = iota(1)
    owner = column(owner_row).astype(jnp.int32)
    earlier = (owner == owner_row) & (iota(0) < lane)
    rank = jnp.sum(earlier.astype(F32), axis=0, keepdims=True)
    for slot in range(2):
        placing = ((iota(0) == owner_row) & (rank == slot)).astype(F32).astype(BF16)
        placing_ref[slot, :, :LINES] = placing
        placing_ref[slot, :, LINES:] = placing


def aim_rows(step, line_row, to_row):
    lane = iota(1)
    line, segment = column(line_row) + 1.0, column(to_row)
    rows = []
    for slot in range(2):
        at = 4 * step + 2 * slot
        rows.append(jnp.where(lane // SEG == at, line, jnp.where(lane // SEG == at + 1, segment, 0.0)).astype(BF16))
    return rows


def aim_codes(aims):
    turned_aims = jnp.transpose(aims)

    def code(at):
        line, segment = turned_aims[SEG * at : SEG * at + 1], turned_aims[SEG * at + SEG : SEG * at + SEG + 1]
        return segment * LINES + line - 1.0

    return [[code(4 * step + 2 * slot) for slot in range(2)] for step in range(STEPS)]


def hit_table(codes, hits_ref):
    place = iota(0).astype(F32)
    for slot in range(2):
        for segment in range(8):
            hit = jnp.where(place + float(segment * LINES) == codes[slot], 0.5, 0.0).astype(BF16)
            for at in (slot, 2 + slot):
                hits_ref[segment * LINES : (segment + 1) * LINES, at * OWNERS : (at + 1) * OWNERS] = hit


def pack_segments(unit, values, pick_ref, group_ref, out_ref):
    parts = [slice(16 * unit, 16 * unit + 8), slice(16 * unit + 8, 16 * unit + 16)]
    for third in range(3):
        halves_of = []
        for part, value in zip(parts, values):
            pick, group = pick_ref[part, :], group_ref[part, :]
            gathered = lane_pick(value[8 * third], pick)
            for s in range(1, 8):
                gathered = jnp.where(group == s, lane_pick(value[8 * third + s], pick), gathered)
            halves_of.append(gathered)
        high, low = halves(jnp.concatenate(halves_of, axis=0))
        columns = slice(third * POINTS, (third + 1) * POINTS)
        out_ref[16 * unit : 16 * unit + 16, columns] = high
        out_ref[LINES + 16 * unit : LINES + 16 * unit + 16, columns] = low


def sending_rows(placing_ref, out_ref, send_ref, rows):
    for slot in range(2):
        sending = dot(placing_ref[slot], out_ref[...])
        for third in range(3):
            send_ref[pl.ds(3 * slot + third, OWNERS, stride=rows), :] = sending[
                :, third * POINTS : (third + 1) * POINTS
            ]


def splicing(received_ref, rows, state_ref, write, parts_ref, hits_ref, gain_ref):
    for slot in range(2):
        highs = slice(slot * OWNERS, (slot + 1) * OWNERS)
        lows = slice((2 + slot) * OWNERS, (3 + slot) * OWNERS)
        for third in range(3):
            high, low = halves(received_ref[pl.ds(3 * slot + third, OWNERS, stride=rows), :])
            parts_ref[highs, third * POINTS : (third + 1) * POINTS] = high
            parts_ref[lows, third * POINTS : (third + 1) * POINTS] = low
        parts_ref[highs, 3 * POINTS :] = jnp.ones((OWNERS, POINTS), BF16)
        parts_ref[lows, 3 * POINTS :] = jnp.zeros((OWNERS, POINTS), BF16)
    gain_ref[...] = dot(hits_ref[...], parts_ref[...]).reshape(8, LINES, 4 * POINTS)
    group = iota(1, (8, POINTS)) // SEG
    bits = [(group & bit) != 0 for bit in (1, 2, 4)]

    def block(at, carry):
        first = pl.multiple_of(8 * at, 8)
        lines = pl.ds(first, 8)
        share = gain_ref[0, lines, 3 * POINTS :]
        for segment in range(1, 8):
            share = jnp.where(group == segment, gain_ref[segment, lines, 3 * POINTS :], share)
        keep = 1.0 - share
        for third in range(3):
            shifted = [gain_ref[segment, lines, third * POINTS : (third + 1) * POINTS] for segment in range(8)]
            for bit, mask in zip((1, 2, 4), bits):
                shifted = [jnp.where(mask, shifted[(i + bit) % 8], shifted[i]) for i in range(8)]
            for s in range(8):
                gained = shifted[-s % 8]
                if s:
                    gained = pltpu.roll(gained, POINTS - SEG * s, 1)
                write(8 * third + s, at, state_ref[8 * third + s, lines, :] * keep + gained)
        return carry

    lax.fori_loop(0, LINES // 8, block, 0, unroll=8)


def means_of(read):
    ones = jnp.full((8, 2 * POINTS), 1.0 / POINTS, BF16)
    rows = []
    for s in range(SPECIES):
        both = jnp.concatenate(halves(read(s)), axis=1)
        sums = lax.dot_general(ones, both, (((1,), (1,)), ((), ())), preferred_element_type=F32)
        rows.append(sums[:1])
    return jnp.concatenate(rows, axis=0)


def scales(diffusivity_row, eigen_row):
    row = jnp.concatenate([diffusivity_row, jnp.zeros((1, POINTS - SPECIES), F32)], axis=1)
    lane = iota(1, (SPECIES, POINTS))
    return jnp.where(lane == 0, 0.5, 1.0 / (1.0 + column(row)[:SPECIES] * eigen_row))


def first_mix_kernel(
    lines_hbm, start_hbm, diffusivity_hbm, eigen_hbm, first_hbm, second_hbm, rates_hbm, frozen_hbm,
    mixed_ref, high_ref, low_ref, scale_ref,
    lines_ref, start_ref, diffusivity_ref, eigen_ref, first_ref, second_ref, rates_ref, frozen_ref, index_ref, sems,
):
    here = [lines_ref.at[third].reshape(LINES, 8, POINTS) for third in range(3)]
    there = [lines_hbm.at[:, pl.ds(8 * third, 8), :] for third in range(3)]
    here += [rates_ref, frozen_ref, diffusivity_ref, eigen_ref, start_ref, first_ref, second_ref]
    there += [rates_hbm, frozen_hbm, diffusivity_hbm, eigen_hbm, start_hbm, first_hbm, second_hbm]
    copies = [pltpu.make_async_copy(a, b, sems.at[i]) for i, (a, b) in enumerate(zip(there, here))]
    for copy in copies:
        copy.start()
    for copy in copies:
        copy.wait()
    mix_tables(rates_ref[...], frozen_ref[...], high_ref, low_ref)
    scale_ref[...] = scales(diffusivity_ref[...], eigen_ref[...])

    def read(s):
        return lines_ref[s // 8, pl.ds(s % 8, LINES, stride=8), :]

    mixing(read, start_ref[0, 0], scale_ref, first_ref, second_ref, mixed_ref, index_ref)


def next_mix_kernel(
    state_ref, start_ref, scale_ref, first_ref, second_ref, from_ref, to_ref, codes_ref,
    mixed_ref, pick_ref, group_ref, hits_ref, index_ref,
):
    mixing(lambda s: state_ref[s], start_ref[1, 0], scale_ref, first_ref, second_ref, mixed_ref, index_ref)
    pick_tables(from_ref[1, 0], to_ref[1, 0], pick_ref, group_ref)
    hit_table([codes_ref[:1], codes_ref[1:2]], hits_ref)


def react(mixed_ref, les_ref, rim_refs, turns_ref, high_ref, low_ref, pick_ref, group_ref, state_ref, mid_ref, out_ref):
    mid = middle(les_ref[:, 0], *[ref[:, 0] for ref in rim_refs])
    mid_ref[...] = mid

    def finish(unit, values):
        pack_segments(unit, values, pick_ref, group_ref, out_ref)

    chemistry(turns_ref, turned(0.5 * mid), high_ref, low_ref, mixed_ref, state_ref, finish)


def first_react_kernel(
    mixed_ref, les_ref, line_even_ref, grid_odd_ref, line_odd_ref, grid_even_ref, high_ref, low_ref, owner_ref, line_ref,
    from_ref, to_ref, counts_ref, state_ref, send_ref, mid_ref, turns_ref, later_ref, out_ref, pick_ref, group_ref,
    placing_ref,
):
    turns_ref[...] = column(counts_ref[0])
    pick_tables(from_ref[0, 0], to_ref[0, 0], pick_ref, group_ref)
    place_tables(owner_ref[0, 0], placing_ref)
    place_tables(owner_ref[1, 0], later_ref)
    aims = [row for step in range(STEPS) for row in aim_rows(step, line_ref[step, 0], to_ref[step, 0])]
    placings = [ref[slot, :, :LINES] for ref in (placing_ref, later_ref) for slot in range(2)]
    rows = ROWS + AIMS
    send_ref[pl.ds(ROWS, OWNERS, stride=rows), :] = dot(
        jnp.concatenate(placings, axis=1), jnp.concatenate(aims, axis=0)
    )
    rim = (grid_even_ref, grid_odd_ref, line_even_ref, line_odd_ref)
    react(mixed_ref, les_ref, rim, turns_ref, high_ref, low_ref, pick_ref, group_ref, state_ref, mid_ref, out_ref)
    sending_rows(placing_ref, out_ref, send_ref, rows)


def next_react_kernel(
    mixed_ref, les_ref, grid_odd_ref, line_odd_ref, grid_even_ref, line_even_ref, high_ref, low_ref, pick_ref, group_ref,
    turns_ref, placing_ref, state_ref, send_ref, mid_ref, out_ref,
):
    rim = (grid_even_ref, grid_odd_ref, line_even_ref, line_odd_ref)
    react(mixed_ref, les_ref, rim, turns_ref, high_ref, low_ref, pick_ref, group_ref, state_ref, mid_ref, out_ref)
    sending_rows(placing_ref, out_ref, send_ref, ROWS)


def next_splice_kernel(received_ref, state_ref, mid_ref, les_ref, lines_ref, codes_ref, parts_ref, gain_ref, hits_ref):
    def write(species, at, value):
        lines_ref[species, pl.ds(pl.multiple_of(8 * at, 8), 8), :] = value

    rows = ROWS + AIMS
    codes = aim_codes(received_ref[pl.ds(ROWS, OWNERS, stride=rows), :])
    codes_ref[...] = jnp.concatenate(codes[1] + [jnp.zeros((6, OWNERS), F32)], axis=0)
    hit_table(codes[0], hits_ref)
    splicing(received_ref, rows, state_ref, write, parts_ref, hits_ref, gain_ref)
    les_ref[:, 0] = 0.5 * mid_ref[...] + 0.5 * means_of(lambda s: lines_ref[s])


def last_splice_kernel(
    received_ref, state_ref, mid_ref, hits_ref, les_ref, lines_hbm, parts_ref, gain_ref, lines_ref, sems
):
    rows = 8 * SPECIES

    def out(at):
        part = pl.ds(pl.multiple_of(at * rows, rows), rows)
        return pltpu.make_async_copy(lines_ref.at[part], lines_hbm.at[part], sems.at[at])

    def write(species, at, value):
        lines_ref[pl.ds(at * rows + species, 8, stride=SPECIES), :] = value
        if species == SPECIES - 1:
            out(at).start()

    splicing(received_ref, ROWS, state_ref, write, parts_ref, hits_ref, gain_ref)
    means = means_of(lambda s: lines_ref[pl.ds(s, LINES, stride=SPECIES), :])
    les_ref[:, 0] = 0.5 * mid_ref[...] + 0.5 * means
    for at in range(LINES // 8):
        out(at).wait()


VMEM = pl.BlockSpec(memory_space=pltpu.VMEM)
HBM = pl.BlockSpec(memory_space=pltpu.HBM)
STATE = jax.ShapeDtypeStruct((SPECIES, LINES, POINTS), F32)
FLAT = jax.ShapeDtypeStruct((LINES * SPECIES, POINTS), F32)
SPLICE_SCRATCH = [pltpu.VMEM((4 * OWNERS, 4 * POINTS), BF16), pltpu.VMEM((8, LINES, 4 * POINTS), F32)]


def call(kernel, inputs, outputs, scratch, micros, in_space=VMEM, out_specs=None):
    size = sum(x.size * x.dtype.itemsize for x in [*inputs, *outputs])
    if in_space is HBM:
        inputs = [pltpu.with_memory_space_constraint(x, pltpu.HBM) for x in inputs]
    return pl.pallas_call(
        kernel,
        out_shape=outputs,
        in_specs=[in_space] * len(inputs),
        out_specs=out_specs or [VMEM] * len(outputs),
        scratch_shapes=scratch,
        cost_estimate=pl.CostEstimate(flops=micros * 10**9, bytes_accessed=size, transcendentals=0),
        compiler_params=pltpu.CompilerParams(vmem_limit_bytes=32 << 20),
    )(*inputs)


def beside(field):
    around = []
    for axis in ("grid", "line"):
        peers = lax.axis_size(axis)
        for start in (0, 1):
            pairs = [(i, (i + 1) % peers) for i in range(start, peers, 2)]
            around.append(lax.ppermute(field, axis, pairs + [(b, a) for a, b in pairs]))
    return around


def body(
    les,
    lines,
    triplet_start,
    splice_owner,
    splice_line,
    splice_from,
    splice_to,
    chem_counts,
    diffusivity,
    rates,
    frozen_inverse,
):
    def shaped(shape, dtype=F32):
        return jax.ShapeDtypeStruct(shape, dtype)

    first_table, second_table, eigen = (jnp.asarray(x) for x in cosine_tables())
    side = SPECIES * 8
    plane = shaped((SPECIES, LINES))
    owner = splice_owner.reshape(STEPS, 1, 1, LINES)
    square = shaped((LINES, POINTS))
    index = shaped((LINES, POINTS), jnp.int32)
    placing = shaped((2, OWNERS, 2 * LINES), BF16)
    hits = shaped((8 * LINES, 4 * OWNERS), BF16)
    scratch_of = lambda x: pltpu.VMEM(x.shape, x.dtype)
    outgoing = pltpu.VMEM((2 * LINES, 3 * POINTS), BF16)

    def exchange(sending):
        sending = sending.reshape(OWNERS, 1, -1)
        received = lax.all_to_all(sending, ("grid", "line"), split_axis=0, concat_axis=0, tiled=True)
        return received.reshape(-1, POINTS)

    grid_even, grid_odd, line_even, line_odd = beside(les)
    inputs = [lines.reshape(LINES, SPECIES, POINTS), triplet_start, diffusivity.reshape(1, SPECIES), eigen]
    inputs += [first_table, second_table, rates, frozen_inverse]
    scratch = [pltpu.VMEM((3, LINES * 8, POINTS), F32)] + [scratch_of(x) for x in inputs[1:]]
    scratch += [scratch_of(index), pltpu.SemaphoreType.DMA((len(inputs) + 2,))]
    table = shaped((side, side), BF16)
    mixed, high, low, scale = call(first_mix_kernel, inputs, [STATE, table, table, plane], scratch, 4, in_space=HBM)

    inputs = [mixed, les, line_even, grid_odd, line_odd, grid_even, high, low, owner, splice_line, splice_from, splice_to, chem_counts]
    outputs = [STATE, shaped((OWNERS * (ROWS + AIMS), POINTS)), plane, square, placing]
    scratch = [outgoing, scratch_of(index), scratch_of(index), scratch_of(placing)]
    state, sending, mid, turns, later = call(first_react_kernel, inputs, outputs, scratch, 6)

    inputs = [exchange(sending), state, mid]
    outputs = [shaped(les.shape), STATE, shaped((8, OWNERS))]
    field, state, codes = call(next_splice_kernel, inputs, outputs, SPLICE_SCRATCH + [scratch_of(hits)], 3)

    grid_even, grid_odd, line_even, line_odd = beside(field)
    inputs = [state, triplet_start, scale, first_table, second_table, splice_from, splice_to, codes]
    mixed, pick, group, landing = call(
        next_mix_kernel, inputs, [STATE, index, index, hits], [scratch_of(index)], 3
    )

    inputs = [mixed, field, grid_odd, line_odd, grid_even, line_even, high, low, pick, group, turns, later]
    outputs = [STATE, shaped((OWNERS * ROWS, POINTS)), plane]
    state, sending, mid = call(next_react_kernel, inputs, outputs, [outgoing], 6)

    inputs = [exchange(sending), state, mid, landing]
    outputs = [shaped(les.shape), FLAT]
    scratch = SPLICE_SCRATCH + [scratch_of(FLAT), pltpu.SemaphoreType.DMA((LINES // 8,))]
    field, state = call(last_splice_kernel, inputs, outputs, scratch, 3, out_specs=[VMEM, HBM])
    return (field, state.reshape(lines.shape))


def solution(mesh):
    in_specs = (
        P(None, "grid", "line"),
        P("grid", "line", None, None, None),
        P(None, "grid", "line", None),
        P(None, "grid", "line", None, None),
        P(None, "grid", "line", None),
        P(None, "grid", "line", None),
        P(None, "grid", "line", None),
        P("grid", "line", None),
        P(),
        P(),
        P(),
    )
    out_specs = (P(None, "grid", "line"), P("grid", "line", None, None, None))
    return jax.shard_map(body, mesh=mesh, in_specs=in_specs, out_specs=out_specs, check_vma=False)
```

```python
import jax
import jax.numpy as jnp
import numpy as np
from jax import lax
from jax.experimental import pallas as pl
from jax.experimental.pallas import tpu as pltpu
from jax.sharding import PartitionSpec as P

SEG = 16
TRIP = 48
KMAX = 6
STEPS = 2
LES_RATE = 0.2
SPECIES = 24
POINTS = 128
LINES = 128
OWNERS = 128
ROWS = 6
AIMS = 1
F32 = jnp.float32
BF16 = jnp.bfloat16


def cosine_tables():
    k = np.arange(POINTS)[:, None]
    p = np.arange(POINTS)[None, :]
    basis = np.sqrt(2.0 / POINTS) * np.cos(np.pi * k * (2 * p + 1) / (2 * POINTS))
    basis[0] = 1.0 / np.sqrt(POINTS)
    tables = []
    for table in (basis.T, basis):
        high = table.astype(BF16)
        low = (table - high.astype(np.float64)).astype(BF16)
        half = np.concatenate([high, low], axis=1)
        tables.append(np.concatenate([half, half], axis=0))
    eigen = 4.0 * np.sin(np.pi * np.arange(POINTS) / (2 * POINTS)) ** 2
    return tables[0], tables[1], eigen.astype(np.float32)[None, :]


def halves(value):
    high = value.astype(BF16)
    return high, (value - high.astype(F32)).astype(BF16)


def dot(a, b):
    return jnp.dot(a, b, preferred_element_type=F32)


def iota(axis, shape=(LINES, POINTS)):
    return lax.broadcasted_iota(jnp.int32, shape, axis)


def column(row):
    return jnp.transpose(jnp.broadcast_to(row.astype(F32), (LINES, POINTS)))


def lane_pick(value, index):
    return jnp.take_along_axis(value, index, axis=1, mode="promise_in_bounds")


def mix_tables(rates, frozen, high_ref, low_ref):
    exact = dict(precision=lax.Precision.HIGHEST, preferred_element_type=F32)
    matrix = jnp.dot(frozen, rates, **exact)
    side = SPECIES * 8
    spread = (iota(0, (side, SPECIES)) // 8 == iota(1, (side, SPECIES))).astype(F32)
    gather = (iota(0, (SPECIES, side)) == iota(1, (SPECIES, side)) // 8).astype(F32)
    wide = jnp.dot(jnp.dot(spread, matrix, **exact), gather, **exact)
    same = iota(0, (side, side)) % 8 == iota(1, (side, side)) % 8
    high, low = halves(jnp.where(same, wide, 0.0))
    high_ref[...] = high
    low_ref[...] = low


def middle(les, grid_even, grid_odd, line_even, line_odd):
    row, place = lax.axis_index("grid"), lax.axis_index("line")
    inner = jnp.logical_and(row > 0, row < lax.axis_size("grid") - 1)
    even = place % 2 == 0
    west = jnp.where(even, line_odd, line_even)
    east = jnp.where(even, line_even, line_odd)
    west = jnp.where(place > 0, west, 0.0)
    east = jnp.where(place < lax.axis_size("line") - 1, east, 0.0)
    lane = iota(1, (SPECIES, LINES))
    left = jnp.where(lane == 0, pltpu.roll(west, 1, 1), pltpu.roll(les, 1, 1))
    right = jnp.where(lane == LINES - 1, pltpu.roll(east, LINES - 1, 1), pltpu.roll(les, LINES - 1, 1))
    return les + LES_RATE * (grid_even + jnp.where(inner, grid_odd, 0.0) + left + right - 4.0 * les)


def turned(value):
    pad = jnp.zeros((POINTS - SPECIES, LINES), F32)
    return jnp.transpose(jnp.concatenate([value, pad], axis=0))


def triplet_index(start):
    place = iota(1)
    start = start.astype(jnp.int32)
    rel = place - start
    third = TRIP // 3
    source = jnp.where(
        rel < third,
        3 * rel,
        jnp.where(rel < 2 * third, 3 * (2 * third - 1 - rel) + 1, 3 * (rel - 2 * third) + 2),
    )
    return jnp.where((rel >= 0) & (rel < TRIP), source + start, place)


def mixing(read, start_row, scale_ref, first_ref, second_ref, state_ref, index_ref):
    index_ref[...] = triplet_index(column(start_row))
    group = 8

    for at in range(SPECIES // group):
        species = [at * group + i for i in range(group)]
        value = jnp.concatenate([lane_pick(read(s), index_ref[...]) for s in species], axis=0)
        wide = dot(jnp.concatenate(halves(value), axis=1), first_ref[...])
        value = wide[:, :POINTS] + wide[:, POINTS:]
        value = value.reshape(group, LINES, POINTS)
        value = jnp.concatenate([value[i] * scale_ref[s : s + 1, :] for i, s in enumerate(species)], axis=0)
        wide = dot(jnp.concatenate(halves(value), axis=1), second_ref[...])
        value = (wide[:, :POINTS] + wide[:, POINTS:]).reshape(group, LINES, POINTS)
        for i, s in enumerate(species):
            state_ref[s] = value[i]


def chemistry(turns_ref, shift, high_ref, low_ref, mixed_ref, state_ref, finish):
    side = SPECIES * 8

    def shifted(part):
        rows = [jnp.broadcast_to(shift[part, s : s + 1], (8, POINTS))[None] for s in range(SPECIES)]
        return mixed_ref[:, part, :] + jnp.concatenate(rows, axis=0)

    for turn in range(KMAX):
        for unit in range(LINES // 16):
            parts = [slice(16 * unit, 16 * unit + 8), slice(16 * unit + 8, 16 * unit + 16)]
            old = [(state_ref[:, part, :] if turn else shifted(part)).reshape(side, POINTS) for part in parts]
            high, low = halves(jnp.tanh(jnp.concatenate(old, axis=1)))
            change = dot(high_ref[...], high) + (dot(low_ref[...], high) + dot(high_ref[...], low))
            done = []
            for at, part in enumerate(parts):
                active = (turns_ref[part, :] > float(turn))[None]
                before = old[at].reshape(SPECIES, 8, POINTS)
                after = before + change[:, at * POINTS : (at + 1) * POINTS].reshape(SPECIES, 8, POINTS)
                done.append(jnp.where(active, after, before))
                state_ref[:, part, :] = done[at]
            if turn == KMAX - 1:
                finish(unit, done)


def pick_tables(from_row, to_row, pick_ref, group_ref):
    lane = iota(1)
    pick_ref[...] = column(from_row).astype(jnp.int32) * SEG + lane % SEG
    group_ref[...] = (lane // SEG - column(to_row).astype(jnp.int32)) & 7


def place_tables(owner_row, placing_ref):
    lane = iota(1)
    owner = column(owner_row).astype(jnp.int32)
    earlier = (owner == owner_row) & (iota(0) < lane)
    rank = jnp.sum(earlier.astype(F32), axis=0, keepdims=True)
    for slot in range(2):
        placing = ((iota(0) == owner_row) & (rank == slot)).astype(F32).astype(BF16)
        placing_ref[slot, :, :LINES] = placing
        placing_ref[slot, :, LINES:] = placing


def aim_rows(step, line_row, to_row):
    lane = iota(1)
    line, segment = column(line_row) + 1.0, column(to_row)
    rows = []
    for slot in range(2):
        at = 4 * step + 2 * slot
        rows.append(jnp.where(lane // SEG == at, line, jnp.where(lane // SEG == at + 1, segment, 0.0)).astype(BF16))
    return rows


def aim_codes(aims):
    turned_aims = jnp.transpose(aims)

    def code(at):
        line, segment = turned_aims[SEG * at : SEG * at + 1], turned_aims[SEG * at + SEG : SEG * at + SEG + 1]
        return segment * LINES + line - 1.0

    return [[code(4 * step + 2 * slot) for slot in range(2)] for step in range(STEPS)]


def hit_table(codes, hits_ref):
    place = iota(0).astype(F32)
    for slot in range(2):
        for segment in range(8):
            hit = jnp.where(place + float(segment * LINES) == codes[slot], 0.5, 0.0).astype(BF16)
            for at in (slot, 2 + slot):
                hits_ref[segment * LINES : (segment + 1) * LINES, at * OWNERS : (at + 1) * OWNERS] = hit


def pack_segments(unit, values, pick_ref, group_ref, out_ref):
    parts = [slice(16 * unit, 16 * unit + 8), slice(16 * unit + 8, 16 * unit + 16)]
    for third in range(3):
        halves_of = []
        for part, value in zip(parts, values):
            pick, group = pick_ref[part, :], group_ref[part, :]
            gathered = lane_pick(value[8 * third], pick)
            for s in range(1, 8):
                gathered = jnp.where(group == s, lane_pick(value[8 * third + s], pick), gathered)
            halves_of.append(gathered)
        high, low = halves(jnp.concatenate(halves_of, axis=0))
        columns = slice(third * POINTS, (third + 1) * POINTS)
        out_ref[16 * unit : 16 * unit + 16, columns] = high
        out_ref[LINES + 16 * unit : LINES + 16 * unit + 16, columns] = low


def sending_rows(placing_ref, out_ref, send_ref, rows):
    sending = dot(placing_ref[...].reshape(2 * OWNERS, 2 * LINES), out_ref[...])
    for slot in range(2):
        for third in range(3):
            send_ref[pl.ds(3 * slot + third, OWNERS, stride=rows), :] = sending[
                slot * OWNERS : (slot + 1) * OWNERS, third * POINTS : (third + 1) * POINTS
            ]


def splicing(received_ref, rows, state_ref, write, parts_ref, hits_ref, gain_ref):
    for slot in range(2):
        highs = slice(slot * OWNERS, (slot + 1) * OWNERS)
        lows = slice((2 + slot) * OWNERS, (3 + slot) * OWNERS)
        for third in range(3):
            high, low = halves(received_ref[pl.ds(3 * slot + third, OWNERS, stride=rows), :])
            parts_ref[highs, third * POINTS : (third + 1) * POINTS] = high
            parts_ref[lows, third * POINTS : (third + 1) * POINTS] = low
        parts_ref[highs, 3 * POINTS :] = jnp.ones((OWNERS, POINTS), BF16)
        parts_ref[lows, 3 * POINTS :] = jnp.zeros((OWNERS, POINTS), BF16)
    gain_ref[...] = dot(hits_ref[...], parts_ref[...]).reshape(8, LINES, 4 * POINTS)
    group = iota(1, (8, POINTS)) // SEG
    bits = [(group & bit) != 0 for bit in (1, 2, 4)]

    def block(at, carry):
        first = pl.multiple_of(8 * at, 8)
        lines = pl.ds(first, 8)
        share = gain_ref[0, lines, 3 * POINTS :]
        for segment in range(1, 8):
            share = jnp.where(group == segment, gain_ref[segment, lines, 3 * POINTS :], share)
        keep = 1.0 - share
        for third in range(3):
            shifted = [gain_ref[segment, lines, third * POINTS : (third + 1) * POINTS] for segment in range(8)]
            for bit, mask in zip((1, 2, 4), bits):
                shifted = [jnp.where(mask, shifted[(i + bit) % 8], shifted[i]) for i in range(8)]
            for s in range(8):
                gained = shifted[-s % 8]
                if s:
                    gained = pltpu.roll(gained, POINTS - SEG * s, 1)
                write(8 * third + s, at, state_ref[8 * third + s, lines, :] * keep + gained)
        return carry

    lax.fori_loop(0, LINES // 8, block, 0, unroll=8)


def means_of(read):
    ones = jnp.full((8, 2 * POINTS), 1.0 / POINTS, BF16)
    rows = []
    for s in range(SPECIES):
        both = jnp.concatenate(halves(read(s)), axis=1)
        sums = lax.dot_general(ones, both, (((1,), (1,)), ((), ())), preferred_element_type=F32)
        rows.append(sums[:1])
    return jnp.concatenate(rows, axis=0)


def scales(diffusivity_row, eigen_row):
    row = jnp.concatenate([diffusivity_row, jnp.zeros((1, POINTS - SPECIES), F32)], axis=1)
    lane = iota(1, (SPECIES, POINTS))
    return jnp.where(lane == 0, 0.5, 1.0 / (1.0 + column(row)[:SPECIES] * eigen_row))


def first_mix_kernel(
    lines_hbm, start_hbm, diffusivity_hbm, eigen_hbm, first_hbm, second_hbm, rates_hbm, frozen_hbm,
    mixed_ref, high_ref, low_ref, scale_ref,
    lines_ref, start_ref, diffusivity_ref, eigen_ref, first_ref, second_ref, rates_ref, frozen_ref, index_ref, sems,
):
    here = [lines_ref.at[third].reshape(LINES, 8, POINTS) for third in range(3)]
    there = [lines_hbm.at[:, pl.ds(8 * third, 8), :] for third in range(3)]
    here += [rates_ref, frozen_ref, diffusivity_ref, eigen_ref, start_ref, first_ref, second_ref]
    there += [rates_hbm, frozen_hbm, diffusivity_hbm, eigen_hbm, start_hbm, first_hbm, second_hbm]
    copies = [pltpu.make_async_copy(a, b, sems.at[i]) for i, (a, b) in enumerate(zip(there, here))]
    for copy in copies:
        copy.start()
    for copy in copies:
        copy.wait()
    mix_tables(rates_ref[...], frozen_ref[...], high_ref, low_ref)
    scale_ref[...] = scales(diffusivity_ref[...], eigen_ref[...])

    def read(s):
        return lines_ref[s // 8, pl.ds(s % 8, LINES, stride=8), :]

    mixing(read, start_ref[0, 0], scale_ref, first_ref, second_ref, mixed_ref, index_ref)


def next_mix_kernel(
    state_ref, start_ref, scale_ref, first_ref, second_ref, from_ref, to_ref, codes_ref,
    mixed_ref, pick_ref, group_ref, hits_ref, index_ref,
):
    mixing(lambda s: state_ref[s], start_ref[1, 0], scale_ref, first_ref, second_ref, mixed_ref, index_ref)
    pick_tables(from_ref[1, 0], to_ref[1, 0], pick_ref, group_ref)
    hit_table([codes_ref[:1], codes_ref[1:2]], hits_ref)


def react(mixed_ref, les_ref, rim_refs, turns_ref, high_ref, low_ref, pick_ref, group_ref, state_ref, mid_ref, out_ref):
    mid = middle(les_ref[:, 0], *[ref[:, 0] for ref in rim_refs])
    mid_ref[...] = mid

    def finish(unit, values):
        pack_segments(unit, values, pick_ref, group_ref, out_ref)

    chemistry(turns_ref, turned(0.5 * mid), high_ref, low_ref, mixed_ref, state_ref, finish)


def first_react_kernel(
    mixed_ref, les_ref, line_even_ref, grid_odd_ref, line_odd_ref, grid_even_ref, high_ref, low_ref, owner_ref, line_ref,
    from_ref, to_ref, counts_ref, state_ref, send_ref, mid_ref, turns_ref, later_ref, out_ref, pick_ref, group_ref,
    placing_ref,
):
    turns_ref[...] = column(counts_ref[0])
    pick_tables(from_ref[0, 0], to_ref[0, 0], pick_ref, group_ref)
    place_tables(owner_ref[0, 0], placing_ref)
    place_tables(owner_ref[1, 0], later_ref)
    aims = [row for step in range(STEPS) for row in aim_rows(step, line_ref[step, 0], to_ref[step, 0])]
    placings = [ref[slot, :, :LINES] for ref in (placing_ref, later_ref) for slot in range(2)]
    rows = ROWS + AIMS
    send_ref[pl.ds(ROWS, OWNERS, stride=rows), :] = dot(
        jnp.concatenate(placings, axis=1), jnp.concatenate(aims, axis=0)
    )
    rim = (grid_even_ref, grid_odd_ref, line_even_ref, line_odd_ref)
    react(mixed_ref, les_ref, rim, turns_ref, high_ref, low_ref, pick_ref, group_ref, state_ref, mid_ref, out_ref)
    sending_rows(placing_ref, out_ref, send_ref, rows)


def next_react_kernel(
    mixed_ref, les_ref, grid_even_ref, line_even_ref, grid_odd_ref, line_odd_ref, high_ref, low_ref, pick_ref, group_ref,
    turns_ref, placing_ref, state_ref, send_ref, mid_ref, out_ref,
):
    rim = (grid_even_ref, grid_odd_ref, line_even_ref, line_odd_ref)
    react(mixed_ref, les_ref, rim, turns_ref, high_ref, low_ref, pick_ref, group_ref, state_ref, mid_ref, out_ref)
    sending_rows(placing_ref, out_ref, send_ref, ROWS)


def next_splice_kernel(received_ref, state_ref, mid_ref, les_ref, lines_ref, codes_ref, parts_ref, gain_ref, hits_ref):
    def write(species, at, value):
        lines_ref[species, pl.ds(pl.multiple_of(8 * at, 8), 8), :] = value

    rows = ROWS + AIMS
    codes = aim_codes(received_ref[pl.ds(ROWS, OWNERS, stride=rows), :])
    codes_ref[...] = jnp.concatenate(codes[1] + [jnp.zeros((6, OWNERS), F32)], axis=0)
    hit_table(codes[0], hits_ref)
    splicing(received_ref, rows, state_ref, write, parts_ref, hits_ref, gain_ref)
    les_ref[:, 0] = 0.5 * mid_ref[...] + 0.5 * means_of(lambda s: lines_ref[s])


def last_splice_kernel(
    received_ref, state_ref, mid_ref, hits_ref, les_ref, lines_hbm, parts_ref, gain_ref, lines_ref, sems
):
    rows = 8 * SPECIES

    def out(at):
        part = pl.ds(pl.multiple_of(at * rows, rows), rows)
        return pltpu.make_async_copy(lines_ref.at[part], lines_hbm.at[part], sems.at[at])

    def write(species, at, value):
        lines_ref[pl.ds(at * rows + species, 8, stride=SPECIES), :] = value
        if species == SPECIES - 1:
            out(at).start()

    splicing(received_ref, ROWS, state_ref, write, parts_ref, hits_ref, gain_ref)
    means = means_of(lambda s: lines_ref[pl.ds(s, LINES, stride=SPECIES), :])
    les_ref[:, 0] = 0.5 * mid_ref[...] + 0.5 * means
    for at in range(LINES // 8):
        out(at).wait()


VMEM = pl.BlockSpec(memory_space=pltpu.VMEM)
HBM = pl.BlockSpec(memory_space=pltpu.HBM)
STATE = jax.ShapeDtypeStruct((SPECIES, LINES, POINTS), F32)
FLAT = jax.ShapeDtypeStruct((LINES * SPECIES, POINTS), F32)
SPLICE_SCRATCH = [pltpu.VMEM((4 * OWNERS, 4 * POINTS), BF16), pltpu.VMEM((8, LINES, 4 * POINTS), F32)]


def call(kernel, inputs, outputs, scratch, micros, in_space=VMEM, out_specs=None):
    size = sum(x.size * x.dtype.itemsize for x in [*inputs, *outputs])
    if in_space is HBM:
        inputs = [pltpu.with_memory_space_constraint(x, pltpu.HBM) for x in inputs]
    return pl.pallas_call(
        kernel,
        out_shape=outputs,
        in_specs=[in_space] * len(inputs),
        out_specs=out_specs or [VMEM] * len(outputs),
        scratch_shapes=scratch,
        cost_estimate=pl.CostEstimate(flops=micros * 10**9, bytes_accessed=size, transcendentals=0),
        compiler_params=pltpu.CompilerParams(vmem_limit_bytes=32 << 20),
    )(*inputs)


def beside(field):
    around = []
    for axis in ("grid", "line"):
        peers = lax.axis_size(axis)
        for start in (0, 1):
            pairs = [(i, (i + 1) % peers) for i in range(start, peers, 2)]
            around.append(lax.ppermute(field, axis, pairs + [(b, a) for a, b in pairs]))
    return around


def body(
    les,
    lines,
    triplet_start,
    splice_owner,
    splice_line,
    splice_from,
    splice_to,
    chem_counts,
    diffusivity,
    rates,
    frozen_inverse,
):
    def shaped(shape, dtype=F32):
        return jax.ShapeDtypeStruct(shape, dtype)

    first_table, second_table, eigen = (jnp.asarray(x) for x in cosine_tables())
    side = SPECIES * 8
    plane = shaped((SPECIES, LINES))
    owner = splice_owner.reshape(STEPS, 1, 1, LINES)
    square = shaped((LINES, POINTS))
    index = shaped((LINES, POINTS), jnp.int32)
    placing = shaped((2, OWNERS, 2 * LINES), BF16)
    hits = shaped((8 * LINES, 4 * OWNERS), BF16)
    scratch_of = lambda x: pltpu.VMEM(x.shape, x.dtype)
    outgoing = pltpu.VMEM((2 * LINES, 3 * POINTS), BF16)

    def exchange(sending):
        sending = sending.reshape(OWNERS, 1, -1)
        received = lax.all_to_all(sending, ("grid", "line"), split_axis=0, concat_axis=0, tiled=True)
        return received.reshape(-1, POINTS)

    grid_even, grid_odd, line_even, line_odd = beside(les)
    inputs = [lines.reshape(LINES, SPECIES, POINTS), triplet_start, diffusivity.reshape(1, SPECIES), eigen]
    inputs += [first_table, second_table, rates, frozen_inverse]
    scratch = [pltpu.VMEM((3, LINES * 8, POINTS), F32)] + [scratch_of(x) for x in inputs[1:]]
    scratch += [scratch_of(index), pltpu.SemaphoreType.DMA((len(inputs) + 2,))]
    table = shaped((side, side), BF16)
    mixed, high, low, scale = call(first_mix_kernel, inputs, [STATE, table, table, plane], scratch, 4, in_space=HBM)

    inputs = [mixed, les, line_even, grid_odd, line_odd, grid_even, high, low, owner, splice_line, splice_from, splice_to, chem_counts]
    outputs = [STATE, shaped((OWNERS * (ROWS + AIMS), POINTS)), plane, square, placing]
    scratch = [outgoing, scratch_of(index), scratch_of(index), scratch_of(placing)]
    state, sending, mid, turns, later = call(first_react_kernel, inputs, outputs, scratch, 6)

    inputs = [exchange(sending), state, mid]
    outputs = [shaped(les.shape), STATE, shaped((8, OWNERS))]
    field, state, codes = call(next_splice_kernel, inputs, outputs, SPLICE_SCRATCH + [scratch_of(hits)], 3)

    grid_even, grid_odd, line_even, line_odd = beside(field)
    inputs = [state, triplet_start, scale, first_table, second_table, splice_from, splice_to, codes]
    mixed, pick, group, landing = call(
        next_mix_kernel, inputs, [STATE, index, index, hits], [scratch_of(index)], 3
    )

    inputs = [mixed, field, grid_even, line_even, grid_odd, line_odd, high, low, pick, group, turns, later]
    outputs = [STATE, shaped((OWNERS * ROWS, POINTS)), plane]
    state, sending, mid = call(next_react_kernel, inputs, outputs, [outgoing], 6)

    inputs = [exchange(sending), state, mid, landing]
    outputs = [shaped(les.shape), FLAT]
    scratch = SPLICE_SCRATCH + [scratch_of(FLAT), pltpu.SemaphoreType.DMA((LINES // 8,))]
    field, state = call(last_splice_kernel, inputs, outputs, scratch, 3, out_specs=[VMEM, HBM])
    return (field, state.reshape(lines.shape))


def solution(mesh):
    in_specs = (
        P(None, "grid", "line"),
        P("grid", "line", None, None, None),
        P(None, "grid", "line", None),
        P(None, "grid", "line", None, None),
        P(None, "grid", "line", None),
        P(None, "grid", "line", None),
        P(None, "grid", "line", None),
        P("grid", "line", None),
        P(),
        P(),
        P(),
    )
    out_specs = (P(None, "grid", "line"), P("grid", "line", None, None, None))
    return jax.shard_map(body, mesh=mesh, in_specs=in_specs, out_specs=out_specs, check_vma=False)
```
